32 devices in a mesh: exp: 8 (over z, x), seq: 4 (over y, core).
Axes of the slice: x: 2, y: 2, z: 4, core: 2. Of those that a mesh axis runs over, the one named last changes fastest.
Arguments:
- out_grad: bfloat16 [4096, 4096], P(('exp', 'seq')), may hold values from -1.5 to 1.5
- chosen: int32 [8, 1024], P('exp'), may hold values from 0 to 4095, as said below
- scores: float32 [8, 1024], P('exp'), may hold values from 0.05 to 1
- saved_pre: bfloat16 [8, 1024, 2, 1536], P('exp', None, None, 'seq'), may hold values from -6 to 6
- gate_up: bfloat16 [8, 4096, 2, 1536], P('exp', None, None, 'seq'), may hold values from -0.09375 to 0.09375
- down: bfloat16 [8, 1536, 4096], P('exp', 'seq'), may hold values from -0.15625 to 0.15625
Outputs:
- in_grad: bfloat16 [4096, 4096], P(('exp', 'seq'))
- score_grad: float32 [8, 1024], P('exp')
The draws below stay inside these ranges and needn't reach their ends.
Inputs may be any that keep to these rules, and one draw needn't show every extreme that they name: `chosen`: each row lists 1024 different tokens. At most 144 of one row's tokens lie in one block of 512 consecutive tokens (the tokens of one index of exp), and every row has exactly 144 in some block.
All inputs are finite; a program needn't handle non-finite values.
Results may differ from the reference program's by a relative error of at most 0.012.
Values may be sent and summed in bfloat16 or wider, within the bound.
A program may use at most 128 MiB of HBM per device.

```python
import math
import jax
import jax.numpy as jnp
from jax import lax

D = 4096
FF = 1536
EXPERTS = 8
TOKENS = 4096
CAP = 1024
GROUP_TOK = 512
GROUP_MOST = 144
N_SEQ = 4


def draw_chosen(key, part):
    base_key = jax.random.fold_in(key, 11)
    key_groups, key_tokens, key_shuffle = jax.random.split(base_key, 3)
    mean_quota = CAP // EXPERTS
    pattern = jnp.array([9, 9, 8, 6], jnp.int32) * mean_quota // 8
    group_scores = jax.random.randint(key_groups, (EXPERTS, EXPERTS), 0, 65536) * EXPERTS + jnp.arange(EXPERTS, dtype=jnp.int32)[None, :]
    group_order = jnp.argsort(group_scores, axis=1)
    group_place = jnp.argsort(group_order, axis=1).astype(jnp.int32)
    group_quota = pattern[group_place % 4]
    token_scores = jax.random.randint(key_tokens, (EXPERTS, EXPERTS, GROUP_TOK), 0, 16384) * GROUP_TOK + jnp.arange(GROUP_TOK, dtype=jnp.int32)[None, None, :]
    candidates = jnp.argsort(token_scores, axis=2)[:, :, :GROUP_MOST].astype(jnp.int32)
    candidates = candidates + (jnp.arange(EXPERTS, dtype=jnp.int32) * GROUP_TOK)[None, :, None]
    usable = (jnp.arange(GROUP_MOST, dtype=jnp.int32)[None, None, :] < group_quota[:, :, None]).astype(jnp.int32)
    flat_tokens = candidates.reshape(EXPERTS, EXPERTS * GROUP_MOST)
    flat_usable = usable.reshape(EXPERTS, EXPERTS * GROUP_MOST)
    shuffle_scores = jax.random.randint(key_shuffle, (EXPERTS, EXPERTS * GROUP_MOST), 0, 32768) * (EXPERTS * GROUP_MOST) + jnp.arange(EXPERTS * GROUP_MOST, dtype=jnp.int32)[None, :]
    shuffle = jnp.argsort(shuffle_scores, axis=1)
    flat_tokens = jnp.take_along_axis(flat_tokens, shuffle, axis=1)
    flat_usable = jnp.take_along_axis(flat_usable, shuffle, axis=1)
    keep_order = jnp.argsort(1 - flat_usable, axis=1, stable=True)[:, :CAP]
    return jnp.take_along_axis(flat_tokens, keep_order, axis=1).astype(jnp.int32)


def block_levels(own_key, dims, pieces, least, top_value):
    def one(position, blocks):
        steps = jax.random.uniform(jax.random.fold_in(jax.random.fold_in(own_key, 6), position), (blocks,), jnp.float32, least / len(pieces), top_value / len(pieces))
        return jnp.repeat(jnp.exp(steps), dims[position] // blocks).reshape((-1,) + (1,) * (len(dims) - position - 1))

    factor_of = one(*pieces[0])
    for cut in pieces[1:]:
        factor_of = factor_of * one(*cut)
    return factor_of


def bell_draw(rng, extent, deviation, bound, cuts=(), kind=jnp.bfloat16):
    loudness = block_levels(rng, extent, cuts, -0.22, 0.18) if cuts else 1.0
    entries = jax.random.normal(rng, extent, jnp.float32) * deviation * loudness
    return jnp.minimum(jnp.maximum(entries, -bound), bound).astype(kind)


def setup_inputs(seed: int = 0) -> dict:
    key_list = jax.random.split(jax.random.key(seed), 7)
    return {
        "out_grad": bell_draw(key_list[0], (TOKENS, D), 0.25, 1.5, ((0, 32),)),
        "chosen": draw_chosen(jax.random.fold_in(key_list[6], 71), 0),
        "scores": jnp.clip(jnp.exp(math.log(1.0) - 2.9957323 * jax.random.uniform(key_list[2], (EXPERTS, CAP), jnp.float32) ** block_levels(key_list[2], (EXPERTS, CAP), ((0, 8),), -0.2, 0.2)), 0.05, 1.0),
        "saved_pre": bell_draw(key_list[3], (EXPERTS, CAP, 2, FF), 1.0, 6.0, ((0, 8), (3, 4))),
        "gate_up": bell_draw(key_list[4], (EXPERTS, D, 2, FF), D ** -0.5, 0.09375, ((0, 8), (3, 4))),
        "down": bell_draw(key_list[5], (EXPERTS, FF, D), FF ** -0.5, 0.15625, ((0, 8), (1, 4))),
    }


def reference(out_grad, chosen, scores, saved_pre, gate_up, down):
    quarter = FF // N_SEQ

    def per_expert(totals, expert_data):
        token_ids, weight, pre, mixing, down_e = expert_data
        dy_rows = out_grad[token_ids]
        back_grad = jnp.dot(dy_rows, down_e.T, preferred_element_type=jnp.float32)
        gate_pre = pre[:, 0].astype(jnp.float32)
        up_pre = pre[:, 1].astype(jnp.float32)
        sigmoid_gate = jax.nn.sigmoid(gate_pre)
        activated = gate_pre * sigmoid_gate
        hidden = (activated * up_pre).astype(jnp.bfloat16)
        hidden = lax.optimization_barrier(hidden)
        score_part = jnp.sum(hidden.astype(jnp.float32) * back_grad, axis=1)
        scaled = weight[:, None] * back_grad
        d_gate = scaled * up_pre * sigmoid_gate * (1.0 + gate_pre * (1.0 - sigmoid_gate))
        d_up = scaled * activated
        d_both = jnp.stack([d_gate, d_up], axis=1).astype(jnp.bfloat16)
        left = d_both.reshape(CAP, 2, N_SEQ, quarter).astype(jnp.float32)
        right = mixing.reshape(D, 2, N_SEQ, quarter).astype(jnp.float32)
        partial_value = jnp.einsum('ckqh,dkqh->qcd', left, right).astype(jnp.bfloat16)
        partial_value = lax.optimization_barrier(partial_value)
        summed = jnp.sum(partial_value.astype(jnp.float32), axis=0)
        totals = totals.at[token_ids].add(summed)
        return totals, score_part

    start = jnp.zeros((TOKENS, D), jnp.float32)
    totals, score_grad = lax.scan(per_expert, start, (chosen, scores, saved_pre, gate_up, down))
    return totals.astype(jnp.bfloat16), score_grad
```

```python
import functools

import jax
import jax.numpy as jnp
from jax import lax
from jax.experimental import pallas as pl
from jax.experimental.pallas import tpu as pltpu
from jax.sharding import PartitionSpec as P

MESH = pl.DeviceIdType.MESH
ANY = pl.BlockSpec(memory_space=pl.ANY)
VMEM = pl.BlockSpec(memory_space=pltpu.VMEM)


def flip(index, bits):
    out, step = index, 1
    while bits >= step:
        if bits & step:
            out = out + step * (1 - 2 * ((index // step) % 2))
        step *= 2
    return out


def greet(peers):
    barrier = pltpu.get_barrier_semaphore()
    for p in peers:
        pl.semaphore_signal(barrier, inc=1, device_id=p, device_id_type=MESH)
    pl.semaphore_wait(barrier, len(peers))


def remote(src, dst, send, recv, to):
    return pltpu.make_async_remote_copy(
        src_ref=src, dst_ref=dst, send_sem=send, recv_sem=recv, device_id=to, device_id_type=MESH
    )


def columns(quarter, width):
    return pl.ds(pl.multiple_of(quarter * width, 128), width)


def exchange_kernel(n_exp, n_seq, chosen, grad, ids, group, send_i, recv_i, send_g, recv_g, local):
    g, s = lax.axis_index("exp"), lax.axis_index("seq")
    width = grad.shape[1] // n_seq
    greet([(flip(g, k), s) for k in range(1, n_exp)] + [(g, flip(s, k)) for k in range(1, n_seq)])
    copies = []
    for k in range(1, n_exp):
        copies.append(remote(chosen, ids.at[g], send_i.at[k], recv_i.at[k], (flip(g, k), s)))
        copies[-1].start()
    for k in range(n_seq - 1, 0, -1):
        t = flip(s, k)
        copies.append(
            remote(grad.at[:, columns(t, width)], group.at[s], send_g.at[k], recv_g.at[k], (g, t))
        )
        copies[-1].start()
    own_ids = pltpu.make_async_copy(chosen, ids.at[g], local.at[0])
    own_grad = pltpu.make_async_copy(grad.at[:, columns(s, width)], group.at[s], local.at[1])
    own_ids.start()
    own_grad.start()
    for c in copies:
        c.wait()
    own_ids.wait()
    own_grad.wait()


def exchange(n_exp, n_seq, chosen, grad):
    rows, width = grad.shape[0], grad.shape[1] // n_seq
    dma = pltpu.SemaphoreType.DMA
    return pl.pallas_call(
        functools.partial(exchange_kernel, n_exp, n_seq),
        out_shape=(
            jax.ShapeDtypeStruct((n_exp,) + chosen.shape, chosen.dtype),
            jax.ShapeDtypeStruct((n_seq, rows, width), grad.dtype),
        ),
        in_specs=[VMEM, VMEM],
        out_specs=(VMEM, VMEM),
        scratch_shapes=[dma((n_exp,)), dma((n_exp,)), dma((n_seq,)), dma((n_seq,)), dma((2,))],
        compiler_params=pltpu.CompilerParams(collective_id=0, has_side_effects=True),
    )(chosen, grad)


def dispatch_kernel(n_exp, out, fetched, s0, r0, sa, ra, sb, rb, sc, rc, local):
    g, s = lax.axis_index("exp"), lax.axis_index("seq")
    width = out.shape[2]
    across, beside = (g, flip(s, 2)), (g, flip(s, 1))
    own, theirs = columns(s, width), columns(flip(s, 2), width)
    greet([(flip(g, k), s) for k in range(1, n_exp)] + [across, beside])
    first = pltpu.make_async_copy(out.at[g], fetched.at[g, :, own], local)
    first.start()
    half = n_exp // 2
    order = []
    for k in range(half):
        order.append(half + k)
        if k:
            order.append(k)
    sends = {}
    for k in order:
        e = flip(g, k)
        sends[k] = remote(out.at[e], fetched.at[g, :, own], s0.at[k], r0.at[k], (e, s))
        sends[k].start()
    crossed, done = [], []
    for k in range(n_exp):
        block = fetched.at[flip(g, k)]
        if k:
            sends[k].wait_recv()
        else:
            first.wait()
        c = remote(block.at[:, own], block.at[:, own], sa.at[k], ra.at[k], across)
        c.start()
        crossed.append(c)
        d = remote(block.at[:, own], block.at[:, own], sb.at[k], rb.at[k], beside)
        d.start()
        done.append(d)
    for k in range(n_exp):
        block = fetched.at[flip(g, k)]
        crossed[k].wait_recv()
        d = remote(block.at[:, theirs], block.at[:, theirs], sc.at[k], rc.at[k], beside)
        d.start()
        done.append(d)
    for k in order:
        sends[k].wait_send()
    for c in crossed:
        c.wait_send()
    for d in done:
        d.wait()


def dispatch(n_exp, n_seq, out):
    rows, width = out.shape[1:]
    dma = pltpu.SemaphoreType.DMA
    return pl.pallas_call(
        functools.partial(dispatch_kernel, n_exp),
        out_shape=jax.ShapeDtypeStruct((n_exp, rows, n_seq * width), out.dtype),
        in_specs=[ANY],
        out_specs=ANY,
        scratch_shapes=[dma((n_exp,))] * 8 + [dma],
        compiler_params=pltpu.CompilerParams(collective_id=1, has_side_effects=True),
    )(out)


def combine_kernel(n_exp, part, arrived, near, sum1, far, sum2, s1, r1, s2, r2, s3, r3, local):
    g, s = lax.axis_index("exp"), lax.axis_index("seq")
    width = arrived.shape[2]
    across, beside = (g, flip(s, 2)), (g, flip(s, 1))
    own, theirs = columns(s, width), columns(flip(s, 2), width)
    greet([(flip(g, k), s) for k in range(1, n_exp)] + [across, beside])
    half = n_exp // 2
    order = list(range(half, n_exp)) + list(range(1, half)) + [0]
    pairs = {}
    for k in order:
        e = flip(g, k)
        pairs[k] = [
            remote(
                part.at[e, :, columns(flip(s, bits), width)],
                near.at[e, i],
                s1.at[k, i],
                r1.at[k, i],
                beside,
            )
            for i, bits in enumerate((3, 1))
        ]
        for c in pairs[k]:
            c.start()
    middle, last = {}, {}
    for k in order:
        e = flip(g, k)
        pairs[k][0].wait_recv()
        both = part[e, :, theirs].astype(jnp.float32) + near[e, 0].astype(jnp.float32)
        sum1[e] = both.astype(jnp.bfloat16)
        middle[k] = remote(sum1.at[e], far.at[e], s2.at[k], r2.at[k], across)
        middle[k].start()
    for k in order:
        e = flip(g, k)
        pairs[k][1].wait_recv()
        middle[k].wait_recv()
        total = part[e, :, own].astype(jnp.float32) + near[e, 1].astype(jnp.float32)
        total = total + far[e].astype(jnp.float32)
        sum2[e] = total.astype(jnp.bfloat16)
        if k:
            last[k] = remote(sum2.at[e], arrived.at[g], s3.at[k], r3.at[k], (e, s))
        else:
            last[k] = pltpu.make_async_copy(sum2.at[e], arrived.at[g], local)
        last[k].start()
    for k in order:
        for c in pairs[k]:
            c.wait_send()
        middle[k].wait_send()
        last[k].wait()


def combine(n_exp, n_seq, part):
    rows, width = part.shape[1], part.shape[2] // n_seq
    dma = pltpu.SemaphoreType.DMA
    block = pltpu.VMEM((n_exp, rows, width), part.dtype)
    return pl.pallas_call(
        functools.partial(combine_kernel, n_exp),
        out_shape=jax.ShapeDtypeStruct((n_exp, rows, width), part.dtype),
        in_specs=[VMEM],
        out_specs=VMEM,
        scratch_shapes=[pltpu.VMEM((n_exp, 2, rows, width), part.dtype), block, block, block]
        + [dma((n_exp, 2))] * 2
        + [dma((n_exp,))] * 4
        + [dma],
        compiler_params=pltpu.CompilerParams(
            collective_id=2, has_side_effects=True, vmem_limit_bytes=48 * 2**20
        ),
    )(part)


def running_count(hits):
    rows, length = hits.shape
    ahead = lax.broadcasted_iota(jnp.int32, (128, 128), 0)
    here = lax.broadcasted_iota(jnp.int32, (128, 128), 1)
    upper = (ahead <= here).astype(jnp.float32).astype(jnp.bfloat16)
    hits = hits.astype(jnp.float32)
    before = jnp.zeros((rows, 1), jnp.float32)
    out = []
    for j in range(length // 128):
        block = hits[:, j * 128 : (j + 1) * 128]
        count = jnp.dot(block.astype(jnp.bfloat16), upper, preferred_element_type=jnp.float32)
        out.append(count + before)
        before = before + jnp.sum(block, axis=1, keepdims=True)
    return jnp.concatenate(out, axis=1)


def plan(n_exp):
    half = n_exp // 2
    order = ["fwd 0", "spread 4", "compute 0", "turn 4", "fwd 1", "compute 4", "spread 5", "gives 0",
             "compute 1", "turn 5", "hand 4", "compute 5", "spread 6", "fwd 2", "gives 1", "compute 2",
             "turn 6", "hand 5", "give 4", "compute 6", "spread 7", "fwd 3", "gives 2", "compute 3",
             "turn 7", "hand 6", "give 5", "gives 3", "compute 7", "score 0", "hand 7", "give 6", "give 7",
             "finish_s 0", "finish_x 0"]
    return [(a.split()[0], int(a.split()[1])) for a in order]


def layer_kernel(
    n_exp, group_tok, grad, chosen, scores, pre, mixing_in, down_in, same_out, cross_out, score_out,
    ids, group, rank, place1, weight, take, take_t, spot, pre_pad, mixing, down,
    fetched, both, part, out_s, out_x, near_s, near, sum1, far, sum2, arrived_s, arrived_x, acc_x,
    score_acc, dma, dma_s, dma_r,
):
    g, s = lax.axis_index("exp"), lax.axis_index("seq")
    half = n_exp // 2
    rows = take.shape[1]
    width = group.shape[2]
    own_tok = group_tok // 4
    hidden_part = down.shape[0]
    y, c = s // 2, s % 2
    hg, pg = g // half, g % half
    across, beside = (g, flip(s, 2)), (g, flip(s, 1))
    own, theirs = columns(s, width), columns(flip(s, 2), width)
    expert_at = [flip(g, k) for k in range(n_exp)]
    seq_at = [flip(s, k) for k in range(4)]
    count = {"n": 0, "local": 0}

    def remote_to(src, dst, to):
        n = count["n"]
        count["n"] = n + 1
        return remote(src, dst, dma_s.at[n], dma_r.at[n], to)

    def local_copy(src, dst):
        n = count["local"]
        count["local"] = n + 1
        return pltpu.make_async_copy(src, dst, dma.at[n])

    get_down = local_copy(down_in, down)
    get_mixing = local_copy(mixing_in, mixing)
    greet([(e, s) for e in expert_at[1:]] + [(g, t) for t in seq_at[1:]])
    id_sends, first, second = [], [], []
    for k in range(1, n_exp):
        id_sends.append(remote_to(chosen, ids.at[g], (expert_at[k], s)))
        id_sends[-1].start()
    mine = pl.ds(pl.multiple_of(s * own_tok, own_tok), own_tok)
    for k in (2, 3, 1):
        t = seq_at[k]
        first.append(remote_to(grad.at[:, columns(t, width)], group.at[t // 2, mine], (g, t)))
        first[-1].start()
    for k in (2, 3, 1):
        t = seq_at[k]
        second.append(
            remote_to(grad.at[:, columns(flip(t, 2), width)], group.at[1 - t // 2, mine], (g, t))
        )
        second[-1].start()
    own_copies = [
        local_copy(chosen, ids.at[g]),
        local_copy(grad.at[:, own], group.at[y, mine]),
        local_copy(grad.at[:, theirs], group.at[1 - y, mine]),
    ]
    for d in own_copies:
        d.start()
    get_down.start()
    get_mixing.start()

    capacity = chosen.shape[1]
    row = lax.broadcasted_iota(jnp.int32, (n_exp, capacity), 0)
    slot = lax.broadcasted_iota(jnp.int32, (rows, capacity), 0).astype(jnp.float32)

    for d in id_sends:
        d.wait_recv()
    own_copies[0].wait()
    local = jnp.zeros((n_exp, capacity), jnp.int32)
    for e in range(n_exp):
        local = jnp.where(row == e, ids[e], local)
    local = local - g * group_tok
    inside = (local >= 0) & (local < group_tok)
    rank[0] = jnp.where(inside, running_count(inside) - 1.0, -1.0)
    rank[1] = (local + 1).astype(jnp.float32)

    @pl.loop(0, n_exp)
    def _(e):
        picked = rank[0, pl.ds(e, 1), :] == slot
        at = jnp.sum(jnp.where(picked, rank[1, pl.ds(e, 1), :], 0.0), axis=1, keepdims=True) - 1.0
        spot[e] = at
        token = lax.broadcasted_iota(jnp.int32, (rows, group_tok), 1).astype(jnp.float32)
        take[e] = (at == token).astype(jnp.float32).astype(jnp.bfloat16)

    def select(e, q):
        return jnp.dot(take[e], group[q], preferred_element_type=jnp.float32).astype(jnp.bfloat16)

    sends, sends_s, moved_s = {}, {}, {}
    for d in first:
        d.wait_recv()
    own_copies[1].wait()
    for k in range(half, n_exp):
        out_x[k - half] = select(expert_at[k], y)
        sends[k] = remote_to(out_x.at[k - half], fetched.at[g, :, own], (expert_at[k], s))
        sends[k].start()

    ids_here = chosen[...]
    low = row * group_tok
    hits = (ids_here >= low) & (ids_here < low + group_tok)
    rank[2] = jnp.where(hits, running_count(hits) - 1.0, -1.0)

    @pl.loop(0, n_exp)
    def _(e):
        picked = rank[2, pl.ds(e, 1), :] == slot
        place1[e] = picked.astype(jnp.float32).astype(jnp.bfloat16)
        weight[e] = jnp.sum(jnp.where(picked, scores[...], 0.0), axis=1, keepdims=True)
        pre_pad[e] = jnp.dot(
            place1[e], pre[...], preferred_element_type=jnp.float32
        ).astype(jnp.bfloat16)

    for d in second:
        d.wait_recv()
    own_copies[2].wait()
    for k in range(half):
        for q in range(2):
            if k:
                out_s[k, :, q * width : (q + 1) * width] = select(expert_at[k], q)
                d = remote_to(
                    out_s.at[k, :, pl.ds(q * width, width)],
                    fetched.at[g, :, columns(2 * q + c, width)],
                    (expert_at[k], s),
                )
                d.start()
                sends_s[k, q] = d
            else:
                fetched[g, :, columns(2 * q + c, width)] = select(g, q)

    @pl.loop(0, 2)
    def _(h):
        at = spot[pl.ds(h * half, half)].reshape(half * rows, 1)
        a = lax.broadcasted_iota(jnp.int32, (half * rows, half * rows), 0)
        b = lax.broadcasted_iota(jnp.int32, (half * rows, half * rows), 1)
        flat = jnp.sum(jnp.where(a == b, at, 0.0), axis=0, keepdims=True)
        token = lax.broadcasted_iota(jnp.int32, (group_tok, half * rows), 0).astype(jnp.float32)
        take_t[h] = (token == flat).astype(jnp.float32).astype(jnp.bfloat16)

    score_acc[...] = jnp.zeros_like(score_acc)
    get_down.wait()
    get_mixing.wait()
    crossed, moved, turned, pairs, middle, last, ends = {}, {}, {}, {}, {}, {}, []
    waited = set()

    def fwd(k):
        moved_s[k] = []
        for q in range(2):
            if k:
                sends_s[k, q].wait_recv()
            block = fetched.at[expert_at[k], :, columns(2 * q + c, width)]
            moved_s[k].append(remote_to(block, block, beside))
            moved_s[k][-1].start()

    def spread(k):
        block = fetched.at[expert_at[k], :, own]
        sends[k].wait_recv()
        crossed[k] = remote_to(block, block, across)
        crossed[k].start()
        moved[k] = remote_to(block, block, beside)
        moved[k].start()

    def turn(k):
        block = fetched.at[expert_at[k], :, theirs]
        crossed[k].wait_recv()
        turned[k] = remote_to(block, block, beside)
        turned[k].start()

    def compute(k):
        e = expert_at[k]
        if k < half:
            for d in moved_s[k]:
                d.wait_recv()
        else:
            moved[k].wait_recv()
            turned[k].wait_recv()
        back = lax.dot_general(
            fetched[e], down[...], (((1,), (1,)), ((), ())), preferred_element_type=jnp.float32
        )
        gate_pre = pre_pad[e, :, :hidden_part].astype(jnp.float32)
        up_pre = pre_pad[e, :, hidden_part:].astype(jnp.float32)
        sigmoid_gate = jax.nn.sigmoid(gate_pre)
        activated = gate_pre * sigmoid_gate
        hidden = (activated * up_pre).astype(jnp.bfloat16)
        value = jnp.sum(hidden.astype(jnp.float32) * back, axis=1, keepdims=True)
        here = place1[e].astype(jnp.float32) > 0.5
        score_acc[...] += jnp.sum(jnp.where(here, value, 0.0), axis=0, keepdims=True)
        scaled = weight[e] * back
        d_gate = scaled * up_pre * sigmoid_gate * (1.0 + gate_pre * (1.0 - sigmoid_gate))
        both[:, :hidden_part] = d_gate.astype(jnp.bfloat16)
        both[:, hidden_part:] = (scaled * activated).astype(jnp.bfloat16)

        @pl.loop(0, mixing.shape[0] // 512)
        def _(i):
            tile = columns(i, 512)
            part[e, :, tile] = lax.dot_general(
                both[...],
                mixing[tile, :],
                (((1,), (1,)), ((), ())),
                preferred_element_type=jnp.float32,
            ).astype(jnp.bfloat16)

        p = e % half
        if k < half:
            pairs[k] = [
                remote_to(
                    part.at[e, :, columns(2 * q + 1 - c, width)],
                    near_s.at[p, :, pl.ds(q * width, width)],
                    beside,
                )
                for q in range(2)
            ]
        else:
            pairs[k] = [
                remote_to(part.at[e, :, columns(flip(s, bits), width)], near.at[p, i], beside)
                for i, bits in enumerate((3, 1))
            ]
        for d in pairs[k]:
            d.start()

    def gives(k):
        e = expert_at[k]
        p = e % half
        if k:
            for q in range(2):
                sends_s[k, q].wait_send()
        for q in range(2):
            pairs[k][q].wait_recv()
            here = pl.ds(q * width, width)
            value = part[e, :, columns(2 * q + c, width)].astype(jnp.float32)
            value = (value + near_s[p, :, here].astype(jnp.float32)).astype(jnp.bfloat16)
            if k:
                out_s[k, :, here] = value
            else:
                arrived_s[pg, :, here] = value
        if k:
            last[k] = remote_to(out_s.at[k], arrived_s.at[pg], (e, s))
            last[k].start()

    def hand(k):
        e = expert_at[k]
        p = e % half
        pairs[k][0].wait_recv()
        value = part[e, :, theirs].astype(jnp.float32) + near[p, 0].astype(jnp.float32)
        sum1[p] = value.astype(jnp.bfloat16)
        middle[k] = remote_to(sum1.at[p], far.at[p], across)
        middle[k].start()

    def give(k):
        e = expert_at[k]
        p = e % half
        pairs[k][1].wait_recv()
        middle[k].wait_recv()
        value = part[e, :, own].astype(jnp.float32) + near[p, 1].astype(jnp.float32)
        value = value + far[p].astype(jnp.float32)
        sum2[p] = value.astype(jnp.bfloat16)
        last[k] = remote_to(sum2.at[p], arrived_x.at[pg], (e, s))
        last[k].start()

    def score(k):
        for j in range(1, 4):
            ends.append(remote_to(score_acc, score_out.at[s], (g, seq_at[j])))
            ends[-1].start()
        ends.append(local_copy(score_acc, score_out.at[s]))
        ends[-1].start()

    def finish_s(k):
        for j in range(1, half):
            last[j].wait_recv()
        for q in range(2):
            terms = arrived_s[:, :, q * width : (q + 1) * width].reshape(half * rows, width)
            group[q] = jnp.dot(
                take_t[hg], terms, preferred_element_type=jnp.float32
            ).astype(jnp.bfloat16)
        for j in (2, 3, 1):
            t = seq_at[j]
            block = pl.ds(pl.multiple_of(t * own_tok, own_tok), own_tok)
            ends.append(remote_to(group.at[:, block], same_out.at[s], (g, t)))
            ends[-1].start()
        ends.append(local_copy(group.at[:, mine], same_out.at[s]))
        ends[-1].start()

    def finish_x(k):
        for j in range(half, n_exp):
            last[j].wait_recv()
        terms = arrived_x[...].reshape(half * rows, width)
        acc_x[...] = jnp.dot(
            take_t[1 - hg], terms, preferred_element_type=jnp.float32
        ).astype(jnp.bfloat16)
        for j in (2, 3, 1):
            t = seq_at[j]
            block = pl.ds(pl.multiple_of(t * own_tok, own_tok), own_tok)
            ends.append(remote_to(acc_x.at[block], cross_out.at[s], (g, t)))
            ends[-1].start()
        ends.append(local_copy(acc_x.at[mine], cross_out.at[s]))
        ends[-1].start()

    steps = {
        "fwd": fwd, "spread": spread, "turn": turn, "compute": compute, "gives": gives,
        "hand": hand, "give": give, "score": score, "finish_s": finish_s, "finish_x": finish_x,
    }
    for step, k in plan(n_exp):
        steps[step](k)
    for d in id_sends + first + second:
        d.wait_send()
    for k in range(n_exp):
        if k < half:
            for d in moved_s[k]:
                d.wait_send()
        else:
            sends[k].wait_send()
            for d in (crossed[k], moved[k], turned[k], middle[k]):
                d.wait_send()
        for d in pairs[k]:
            d.wait_send()
        if k:
            last[k].wait_send()
    for d in ends:
        d.wait()


def layer(n_exp, out_grad, chosen, scores, pre, mixing, down):
    own_tok, model_width = out_grad.shape
    capacity = chosen.shape[1]
    width = model_width // 4
    group_tok = own_tok * 4
    rows = 9 * capacity // (8 * n_exp)
    half = n_exp // 2
    hidden2 = mixing.shape[1]
    kind = out_grad.dtype
    dma = pltpu.SemaphoreType.DMA
    f32 = jnp.float32

    def v(*shape, dtype=kind):
        return pltpu.VMEM(shape, dtype)

    total = 17 * n_exp + 40
    return pl.pallas_call(
        functools.partial(layer_kernel, n_exp, group_tok),
        out_shape=(
            jax.ShapeDtypeStruct((4, 2, own_tok, width), kind),
            jax.ShapeDtypeStruct((4, own_tok, width), kind),
            jax.ShapeDtypeStruct((4, 1, capacity), f32),
        ),
        in_specs=[ANY, VMEM, VMEM, VMEM, ANY, ANY],
        out_specs=(ANY, ANY, VMEM),
        scratch_shapes=[
            v(n_exp, 1, capacity, dtype=jnp.int32),
            v(2, group_tok, width),
            v(3, n_exp, capacity, dtype=f32),
            v(n_exp, rows, capacity),
            v(n_exp, rows, 1, dtype=f32),
            v(n_exp, rows, group_tok),
            v(2, group_tok, half * rows),
            v(n_exp, rows, 1, dtype=f32),
            v(n_exp, rows, hidden2),
            v(model_width, hidden2),
            v(hidden2 // 2, model_width),
            v(n_exp, rows, model_width),
            v(rows, hidden2),
            v(n_exp, rows, model_width),
            v(half, rows, 2 * width),
            v(half, rows, width),
            v(half, rows, 2 * width),
            v(half, 2, rows, width),
            v(half, rows, width),
            v(half, rows, width),
            v(half, rows, width),
            v(half, rows, 2 * width),
            v(half, rows, width),
            v(group_tok, width),
            v(1, capacity, dtype=f32),
            dma((8,)),
            dma((total,)),
            dma((total,)),
        ],
        compiler_params=pltpu.CompilerParams(
            collective_id=4, has_side_effects=True, vmem_limit_bytes=60 * 2**20
        ),
    )(out_grad, chosen, scores, pre, mixing, down)


def regroup_kernel(
    n_seq, totals, score, out, score_sum, scores, send, recv, send_s, recv_s, local
):
    g, s = lax.axis_index("exp"), lax.axis_index("seq")
    width = totals.shape[2]
    own = columns(s, width)
    greet([(g, flip(s, k)) for k in range(1, n_seq)])
    copies = []
    for k in range(n_seq - 1, 0, -1):
        t = flip(s, k)
        copies.append(remote(totals.at[t], out.at[:, own], send.at[k], recv.at[k], (g, t)))
        copies[-1].start()
        copies.append(remote(score, scores.at[s], send_s.at[k], recv_s.at[k], (g, t)))
        copies[-1].start()
    mine = pltpu.make_async_copy(totals.at[s], out.at[:, own], local)
    mine.start()
    scores[s] = score[...]
    for c in copies:
        c.wait()
    value = scores[0]
    for k in range(1, n_seq):
        value = value + scores[k]
    score_sum[...] = value
    mine.wait()


def regroup(n_seq, totals, score):
    rows, width = totals.shape[1:]
    dma = pltpu.SemaphoreType.DMA
    return pl.pallas_call(
        functools.partial(regroup_kernel, n_seq),
        out_shape=(
            jax.ShapeDtypeStruct((rows, n_seq * width), totals.dtype),
            jax.ShapeDtypeStruct(score.shape, score.dtype),
        ),
        in_specs=[VMEM, VMEM],
        out_specs=(VMEM, VMEM),
        scratch_shapes=[pltpu.VMEM((n_seq,) + score.shape, score.dtype)]
        + [dma((n_seq,))] * 4
        + [dma],
        compiler_params=pltpu.CompilerParams(collective_id=3, has_side_effects=True),
    )(totals, score)


def counts(hits):
    length = hits.shape[1]
    at = jnp.arange(length, dtype=jnp.int32)
    upper = (at[:, None] <= at[None, :]).astype(jnp.bfloat16)
    total = jnp.dot(hits.astype(jnp.bfloat16), upper, preferred_element_type=jnp.float32)
    return total.astype(jnp.int32)


def local(out_grad, chosen, scores, saved_pre, gate_up, down):
    n_exp = lax.axis_size("exp")
    n_seq = lax.axis_size("seq")
    capacity = chosen.shape[1]
    slot_most = 9 * capacity // (8 * n_exp)
    tok_count, model_width = out_grad.shape
    width = model_width // n_seq
    group_tok = tok_count * n_seq
    pad_rows = n_exp * slot_most
    hidden_part = gate_up.shape[3]
    group_index = lax.axis_index("exp")

    if slot_most % 16 == 0 and n_exp >= 4 and n_seq == 4:
        same, cross, score_parts = layer(
            n_exp,
            out_grad,
            chosen,
            scores,
            saved_pre[0].reshape(capacity, 2 * hidden_part),
            gate_up[0].reshape(model_width, 2 * hidden_part),
            down[0],
        )
        quarters = []
        for q in range(4):
            value = same[q % 2, q // 2].astype(jnp.float32) + same[2 + q % 2, q // 2].astype(
                jnp.float32
            )
            quarters.append((value + cross[q].astype(jnp.float32)).astype(jnp.bfloat16))
        return jnp.concatenate(quarters, axis=1), jnp.sum(score_parts, axis=0)

    own_ids = chosen[0]
    owner_group = own_ids // group_tok
    owner_hits = (owner_group[None, :] == jnp.arange(n_exp, dtype=jnp.int32)[:, None]).astype(
        jnp.int32
    )
    slot_order = jnp.sum(counts(owner_hits) * owner_hits, axis=0) - 1
    position = owner_group * slot_most + slot_order
    place = position[None, :] == jnp.arange(pad_rows, dtype=jnp.int32)[:, None]
    weight_padded = jnp.sum(jnp.where(place, scores[0][None, :], 0.0), axis=1)
    place_one = place.astype(jnp.bfloat16)

    def padded(x):
        return jnp.dot(place_one, x, preferred_element_type=jnp.float32)

    gate_pre = padded(saved_pre[0, :, 0])
    up_pre = padded(saved_pre[0, :, 1])
    mixing = gate_up[0].reshape(model_width, 2 * hidden_part)

    ids, group = exchange(n_exp, n_seq, chosen.reshape(capacity // 128, 128), out_grad)
    local_ids = ids.reshape(n_exp, capacity) - group_index * group_tok
    inside = (local_ids >= 0) & (local_ids < group_tok)
    slot_rank = counts(inside) - 1
    slot_ids = jnp.arange(slot_most, dtype=jnp.int32)
    picked = inside[:, None, :] & (slot_rank[:, None, :] == slot_ids[None, :, None])
    source = jnp.sum(jnp.where(picked, local_ids[:, None, :] + 1, 0), axis=2).reshape(pad_rows) - 1
    tokens = jnp.arange(group_tok, dtype=jnp.int32)
    take = (source[:, None] == tokens[None, :]).astype(jnp.bfloat16)
    outgoing = jnp.dot(
        take, group.reshape(group_tok, width), preferred_element_type=jnp.float32
    ).astype(jnp.bfloat16)
    outgoing = outgoing.reshape(n_exp, slot_most, width)
    fetched = dispatch(n_exp, n_seq, outgoing)
    fetched = fetched.reshape(pad_rows, model_width)

    back_grad = lax.dot_general(
        fetched, down[0], (((1,), (1,)), ((), ())), preferred_element_type=jnp.float32
    )
    sigmoid_gate = jax.nn.sigmoid(gate_pre)
    activated = gate_pre * sigmoid_gate
    hidden = (activated * up_pre).astype(jnp.bfloat16)
    hidden = lax.optimization_barrier(hidden)
    score_part = jnp.sum(hidden.astype(jnp.float32) * back_grad, axis=1)
    scaled = weight_padded[:, None] * back_grad
    d_gate = scaled * up_pre * sigmoid_gate * (1.0 + gate_pre * (1.0 - sigmoid_gate))
    d_up = scaled * activated
    d_both = jnp.concatenate([d_gate, d_up], axis=1).astype(jnp.bfloat16)
    partial_value = lax.dot_general(
        d_both, mixing, (((1,), (1,)), ((), ())), preferred_element_type=jnp.float32
    ).astype(jnp.bfloat16)
    arrived = combine(n_exp, n_seq, partial_value.reshape(n_exp, slot_most, model_width))
    score_slots = jnp.sum(jnp.where(place, score_part[:, None], 0.0), axis=0)
    totals = lax.dot_general(
        take,
        arrived.reshape(pad_rows, width),
        (((0,), (0,)), ((), ())),
        preferred_element_type=jnp.float32,
    ).astype(jnp.bfloat16)
    summed, score_grad = regroup(
        n_seq,
        totals.reshape(n_seq, tok_count, width),
        score_slots.reshape(capacity // 128, 128),
    )
    return (summed, score_grad.reshape(1, capacity))


def solution(mesh):
    return jax.shard_map(
        local,
        mesh=mesh,
        in_specs=(
            P(("exp", "seq"), None),
            P("exp", None),
            P("exp", None),
            P("exp", None, None, "seq"),
            P("exp", None, None, "seq"),
            P("exp", "seq", None),
        ),
        out_specs=(P(("exp", "seq"), None), P("exp", None)),
        check_vma=False,
    )
```

```python
import functools

import jax
import jax.numpy as jnp
from jax import lax
from jax.experimental import pallas as pl
from jax.experimental.pallas import tpu as pltpu
from jax.sharding import PartitionSpec as P

MESH = pl.DeviceIdType.MESH
ANY = pl.BlockSpec(memory_space=pl.ANY)
VMEM = pl.BlockSpec(memory_space=pltpu.VMEM)


def flip(index, bits):
    out, step = index, 1
    while bits >= step:
        if bits & step:
            out = out + step * (1 - 2 * ((index // step) % 2))
        step *= 2
    return out


def greet(peers):
    barrier = pltpu.get_barrier_semaphore()
    for p in peers:
        pl.semaphore_signal(barrier, inc=1, device_id=p, device_id_type=MESH)
    pl.semaphore_wait(barrier, len(peers))


def remote(src, dst, send, recv, to):
    return pltpu.make_async_remote_copy(
        src_ref=src, dst_ref=dst, send_sem=send, recv_sem=recv, device_id=to, device_id_type=MESH
    )


def columns(quarter, width):
    return pl.ds(pl.multiple_of(quarter * width, 128), width)


def exchange_kernel(n_exp, n_seq, chosen, grad, ids, group, send_i, recv_i, send_g, recv_g, local):
    g, s = lax.axis_index("exp"), lax.axis_index("seq")
    width = grad.shape[1] // n_seq
    greet([(flip(g, k), s) for k in range(1, n_exp)] + [(g, flip(s, k)) for k in range(1, n_seq)])
    copies = []
    for k in range(1, n_exp):
        copies.append(remote(chosen, ids.at[g], send_i.at[k], recv_i.at[k], (flip(g, k), s)))
        copies[-1].start()
    for k in range(n_seq - 1, 0, -1):
        t = flip(s, k)
        copies.append(
            remote(grad.at[:, columns(t, width)], group.at[s], send_g.at[k], recv_g.at[k], (g, t))
        )
        copies[-1].start()
    own_ids = pltpu.make_async_copy(chosen, ids.at[g], local.at[0])
    own_grad = pltpu.make_async_copy(grad.at[:, columns(s, width)], group.at[s], local.at[1])
    own_ids.start()
    own_grad.start()
    for c in copies:
        c.wait()
    own_ids.wait()
    own_grad.wait()


def exchange(n_exp, n_seq, chosen, grad):
    rows, width = grad.shape[0], grad.shape[1] // n_seq
    dma = pltpu.SemaphoreType.DMA
    return pl.pallas_call(
        functools.partial(exchange_kernel, n_exp, n_seq),
        out_shape=(
            jax.ShapeDtypeStruct((n_exp,) + chosen.shape, chosen.dtype),
            jax.ShapeDtypeStruct((n_seq, rows, width), grad.dtype),
        ),
        in_specs=[VMEM, VMEM],
        out_specs=(VMEM, VMEM),
        scratch_shapes=[dma((n_exp,)), dma((n_exp,)), dma((n_seq,)), dma((n_seq,)), dma((2,))],
        compiler_params=pltpu.CompilerParams(collective_id=0, has_side_effects=True),
    )(chosen, grad)


def dispatch_kernel(n_exp, out, fetched, s0, r0, sa, ra, sb, rb, sc, rc, local):
    g, s = lax.axis_index("exp"), lax.axis_index("seq")
    width = out.shape[2]
    across, beside = (g, flip(s, 2)), (g, flip(s, 1))
    own, theirs = columns(s, width), columns(flip(s, 2), width)
    greet([(flip(g, k), s) for k in range(1, n_exp)] + [across, beside])
    first = pltpu.make_async_copy(out.at[g], fetched.at[g, :, own], local)
    first.start()
    half = n_exp // 2
    order = []
    for k in range(half):
        order.append(half + k)
        if k:
            order.append(k)
    sends = {}
    for k in order:
        e = flip(g, k)
        sends[k] = remote(out.at[e], fetched.at[g, :, own], s0.at[k], r0.at[k], (e, s))
        sends[k].start()
    crossed, done = [], []
    for k in range(n_exp):
        block = fetched.at[flip(g, k)]
        if k:
            sends[k].wait_recv()
        else:
            first.wait()
        c = remote(block.at[:, own], block.at[:, own], sa.at[k], ra.at[k], across)
        c.start()
        crossed.append(c)
        d = remote(block.at[:, own], block.at[:, own], sb.at[k], rb.at[k], beside)
        d.start()
        done.append(d)
    for k in range(n_exp):
        block = fetched.at[flip(g, k)]
        crossed[k].wait_recv()
        d = remote(block.at[:, theirs], block.at[:, theirs], sc.at[k], rc.at[k], beside)
        d.start()
        done.append(d)
    for k in order:
        sends[k].wait_send()
    for c in crossed:
        c.wait_send()
    for d in done:
        d.wait()


def dispatch(n_exp, n_seq, out):
    rows, width = out.shape[1:]
    dma = pltpu.SemaphoreType.DMA
    return pl.pallas_call(
        functools.partial(dispatch_kernel, n_exp),
        out_shape=jax.ShapeDtypeStruct((n_exp, rows, n_seq * width), out.dtype),
        in_specs=[ANY],
        out_specs=ANY,
        scratch_shapes=[dma((n_exp,))] * 8 + [dma],
        compiler_params=pltpu.CompilerParams(collective_id=1, has_side_effects=True),
    )(out)


def combine_kernel(n_exp, part, arrived, near, sum1, far, sum2, s1, r1, s2, r2, s3, r3, local):
    g, s = lax.axis_index("exp"), lax.axis_index("seq")
    width = arrived.shape[2]
    across, beside = (g, flip(s, 2)), (g, flip(s, 1))
    own, theirs = columns(s, width), columns(flip(s, 2), width)
    greet([(flip(g, k), s) for k in range(1, n_exp)] + [across, beside])
    half = n_exp // 2
    order = list(range(half, n_exp)) + list(range(1, half)) + [0]
    pairs = {}
    for k in order:
        e = flip(g, k)
        pairs[k] = [
            remote(
                part.at[e, :, columns(flip(s, bits), width)],
                near.at[e, i],
                s1.at[k, i],
                r1.at[k, i],
                beside,
            )
            for i, bits in enumerate((3, 1))
        ]
        for c in pairs[k]:
            c.start()
    middle, last = {}, {}
    for k in order:
        e = flip(g, k)
        pairs[k][0].wait_recv()
        both = part[e, :, theirs].astype(jnp.float32) + near[e, 0].astype(jnp.float32)
        sum1[e] = both.astype(jnp.bfloat16)
        middle[k] = remote(sum1.at[e], far.at[e], s2.at[k], r2.at[k], across)
        middle[k].start()
    for k in order:
        e = flip(g, k)
        pairs[k][1].wait_recv()
        middle[k].wait_recv()
        total = part[e, :, own].astype(jnp.float32) + near[e, 1].astype(jnp.float32)
        total = total + far[e].astype(jnp.float32)
        sum2[e] = total.astype(jnp.bfloat16)
        if k:
            last[k] = remote(sum2.at[e], arrived.at[g], s3.at[k], r3.at[k], (e, s))
        else:
            last[k] = pltpu.make_async_copy(sum2.at[e], arrived.at[g], local)
        last[k].start()
    for k in order:
        for c in pairs[k]:
            c.wait_send()
        middle[k].wait_send()
        last[k].wait()


def combine(n_exp, n_seq, part):
    rows, width = part.shape[1], part.shape[2] // n_seq
    dma = pltpu.SemaphoreType.DMA
    block = pltpu.VMEM((n_exp, rows, width), part.dtype)
    return pl.pallas_call(
        functools.partial(combine_kernel, n_exp),
        out_shape=jax.ShapeDtypeStruct((n_exp, rows, width), part.dtype),
        in_specs=[VMEM],
        out_specs=VMEM,
        scratch_shapes=[pltpu.VMEM((n_exp, 2, rows, width), part.dtype), block, block, block]
        + [dma((n_exp, 2))] * 2
        + [dma((n_exp,))] * 4
        + [dma],
        compiler_params=pltpu.CompilerParams(
            collective_id=2, has_side_effects=True, vmem_limit_bytes=48 * 2**20
        ),
    )(part)


def running_count(hits):
    rows, length = hits.shape
    ahead = lax.broadcasted_iota(jnp.int32, (128, 128), 0)
    here = lax.broadcasted_iota(jnp.int32, (128, 128), 1)
    upper = (ahead <= here).astype(jnp.float32).astype(jnp.bfloat16)
    hits = hits.astype(jnp.float32)
    before = jnp.zeros((rows, 1), jnp.float32)
    out = []
    for j in range(length // 128):
        block = hits[:, j * 128 : (j + 1) * 128]
        count = jnp.dot(block.astype(jnp.bfloat16), upper, preferred_element_type=jnp.float32)
        out.append(count + before)
        before = before + jnp.sum(block, axis=1, keepdims=True)
    return jnp.concatenate(out, axis=1)


ORDER = [
    "csend 4 0", "mix 0", "mix 1", "csend 4 1", "csend 5 0", "csend 5 1", "spread 4 0", "place",
    "spread 4 1", "ssend 1", "ssend 2", "csend 6 0", "csend 6 1", "ssend 3", "csend 7 0",
    "csend 7 1", "ssend 0", "fwd 0", "turn 4 0", "mix 2", "mix 3", "spread 5 0", "turn 4 1",
    "mix 4", "mix 5", "spread 5 1", "mix 6", "mix 7", "fwd 1", "mix 8", "mix 9", "ready",
    "compute 4", "turn 5 0", "turn 5 1", "compute 0", "hand 4 0", "hand 4 1", "taket", "spread 6 0",
    "compute 5", "gives 0", "fwd 2", "spread 6 1", "compute 1", "give 4 0", "give 4 1", "hand 5 0",
    "hand 5 1", "turn 6 0", "turn 6 1", "gives 1", "compute 2", "spread 7 0", "compute 6",
    "give 5 0", "give 5 1", "hand 6 0", "hand 6 1", "gives 2", "fwd 3", "compute 3", "spread 7 1",
    "turn 7 0", "turn 7 1", "gives 3", "compute 7", "score", "hand 7 0", "hand 7 1", "give 6 0",
    "give 7 0", "give 6 1", "give 7 1", "finish_s", "finish_x 0", "finish_x 1",
]


def plan():
    for step in ORDER:
        name, *numbers = step.split()
        yield name, [int(n) for n in numbers]


def layer_kernel(
    n_exp, group_tok, grad, chosen, scores, pre_in, mixing_in, down_in, same_out, cross_out, score_out,
    ids, group, rank, place1, weight, take, take_t, spot, pre, pre_pad, mixing, down, raw,
    fetched, both, part, out_s, out_x, near_s, near, far, sum2, arrived_s, arrived_x, acc_x,
    score_acc, dma, dma_s, dma_r,
):
    g, s = lax.axis_index("exp"), lax.axis_index("seq")
    half = n_exp // 2
    rows = take.shape[1]
    width = group.shape[2]
    own_tok = group_tok // 4
    hw = width // 2
    hidden_part = down.shape[0]
    y, c = s // 2, s % 2
    hg, pg = g // half, g % half
    across, beside = (g, flip(s, 2)), (g, flip(s, 1))
    own, theirs = columns(s, width), columns(flip(s, 2), width)
    expert_at = [flip(g, k) for k in range(n_exp)]
    seq_at = [flip(s, k) for k in range(4)]
    count = {"n": 0, "local": 0}
    halves = [pl.ds(h * hw, hw) for h in range(2)]

    def cols(quarter, h):
        return pl.ds(pl.multiple_of(quarter * width + h * hw, 128), hw)

    def remote_to(src, dst, to):
        n = count["n"]
        count["n"] = n + 1
        return remote(src, dst, dma_s.at[n], dma_r.at[n], to)

    def local_copy(src, dst):
        n = count["local"]
        count["local"] = n + 1
        return pltpu.make_async_copy(src, dst, dma.at[n])

    get_down = local_copy(down_in, down)
    step_rows = raw.shape[1]
    raw_parts = [(src, dst, i) for src, dst in ((pre_in, pre), (mixing_in, mixing))
                 for i in range(dst.shape[0] // step_rows)]
    raw_copies = [
        local_copy(src.at[pl.ds(i * step_rows, step_rows)], raw.at[n % 2])
        for n, (src, _, i) in enumerate(raw_parts)
    ]
    greet([(e, s) for e in expert_at[1:]] + [(g, t) for t in seq_at[1:]])
    id_sends, first, second = [], {}, []
    for k in range(1, n_exp):
        id_sends.append(remote_to(chosen, ids.at[g], (expert_at[k], s)))
        id_sends[-1].start()
    mine = pl.ds(pl.multiple_of(s * own_tok, own_tok), own_tok)
    for h in range(2):
        for k in (2, 3, 1):
            t = seq_at[k]
            first[k, h] = remote_to(
                grad.at[:, cols(t, h)], group.at[t // 2, mine, halves[h]], (g, t)
            )
            first[k, h].start()
    for k in (2, 3, 1):
        t = seq_at[k]
        second.append(
            remote_to(grad.at[:, columns(flip(t, 2), width)], group.at[1 - t // 2, mine], (g, t))
        )
        second[-1].start()
    own_copies = [
        local_copy(chosen, ids.at[g]),
        local_copy(grad.at[:, own], group.at[y, mine]),
        local_copy(grad.at[:, theirs], group.at[1 - y, mine]),
    ]
    for d in own_copies:
        d.start()
    get_down.start()
    raw_copies[0].start()

    capacity = chosen.shape[1]
    row = lax.broadcasted_iota(jnp.int32, (n_exp, capacity), 0)
    slot = lax.broadcasted_iota(jnp.int32, (rows, capacity), 0).astype(jnp.float32)

    for d in id_sends:
        d.wait_recv()
    own_copies[0].wait()
    local = jnp.zeros((n_exp, capacity), jnp.int32)
    for e in range(n_exp):
        local = jnp.where(row == e, ids[e], local)
    local = local - g * group_tok
    inside = (local >= 0) & (local < group_tok)
    rank[0] = jnp.where(inside, running_count(inside) - 1.0, -1.0)
    rank[1] = (local + 1).astype(jnp.float32)

    @pl.loop(0, n_exp)
    def _(e):
        picked = rank[0, pl.ds(e, 1), :] == slot
        at = jnp.sum(jnp.where(picked, rank[1, pl.ds(e, 1), :], 0.0), axis=1, keepdims=True) - 1.0
        spot[e] = at
        token = lax.broadcasted_iota(jnp.int32, (rows, group_tok), 1).astype(jnp.float32)
        take[e] = (at == token).astype(jnp.float32).astype(jnp.bfloat16)

    def select(e, q):
        return jnp.dot(take[e], group[q], preferred_element_type=jnp.float32).astype(jnp.bfloat16)

    sends, sends_s, moved_s = {}, {}, {}
    crossed, moved, turned, pairs, middle, last, ends = {}, {}, {}, {}, {}, {}, []
    seen = set()
    score_acc[...] = jnp.zeros_like(score_acc)

    def once(*key):
        new = key not in seen
        seen.add(key)
        return new

    def csend(k, h):
        if once("own"):
            own_copies[1].wait()
        if once("first", h):
            for j in (2, 3, 1):
                first[j, h].wait_recv()
        e = expert_at[k]
        out_x[k - half, :, halves[h]] = jnp.dot(
            take[e], group[y, :, halves[h]], preferred_element_type=jnp.float32
        ).astype(jnp.bfloat16)
        sends[k, h] = remote_to(
            out_x.at[k - half, :, halves[h]], fetched.at[g, :, cols(s, h)], (e, s)
        )
        sends[k, h].start()

    def ssend(k):
        if once("second"):
            for d in second:
                d.wait_recv()
            own_copies[2].wait()
        for q in range(2):
            if k:
                out_s[k, :, q * width : (q + 1) * width] = select(expert_at[k], q)
                sends_s[k, q] = remote_to(
                    out_s.at[k, :, pl.ds(q * width, width)],
                    fetched.at[g, :, columns(2 * q + c, width)],
                    (expert_at[k], s),
                )
                sends_s[k, q].start()
            else:
                fetched[g, :, columns(2 * q + c, width)] = select(g, q)

    def mix(n):
        if n + 1 < len(raw_copies):
            raw_copies[n + 1].start()
        raw_copies[n].wait()
        _, dst, i = raw_parts[n]
        dst[i * step_rows : (i + 1) * step_rows, :] = raw[n % 2].reshape(
            step_rows, 2 * hidden_part
        )

    def place():
        ids_here = chosen[...]
        low = row * group_tok
        hits = (ids_here >= low) & (ids_here < low + group_tok)
        rank[2] = jnp.where(hits, running_count(hits) - 1.0, -1.0)

        @pl.loop(0, n_exp)
        def _(e):
            picked = rank[2, pl.ds(e, 1), :] == slot
            place1[e] = picked.astype(jnp.float32).astype(jnp.bfloat16)
            weight[e] = jnp.sum(jnp.where(picked, scores[...], 0.0), axis=1, keepdims=True)
            pre_pad[e] = jnp.dot(
                place1[e], pre[...], preferred_element_type=jnp.float32
            ).astype(jnp.bfloat16)

    def taket():
        @pl.loop(0, 2)
        def _(h):
            at = spot[pl.ds(h * half, half)].reshape(half * rows, 1)
            a = lax.broadcasted_iota(jnp.int32, (half * rows, half * rows), 0)
            b = lax.broadcasted_iota(jnp.int32, (half * rows, half * rows), 1)
            flat = jnp.sum(jnp.where(a == b, at, 0.0), axis=0, keepdims=True)
            token = lax.broadcasted_iota(jnp.int32, (group_tok, half * rows), 0)
            token = token.astype(jnp.float32)
            take_t[h] = (token == flat).astype(jnp.float32).astype(jnp.bfloat16)

    def ready():
        get_down.wait()

    def fwd(k):
        moved_s[k] = []
        for q in range(2):
            if k:
                sends_s[k, q].wait_recv()
            block = fetched.at[expert_at[k], :, columns(2 * q + c, width)]
            moved_s[k].append(remote_to(block, block, beside))
            moved_s[k][-1].start()

    def spread(k, h):
        block = fetched.at[expert_at[k], :, cols(s, h)]
        sends[k, h].wait_recv()
        crossed[k, h] = remote_to(block, block, across)
        crossed[k, h].start()
        moved[k, h] = remote_to(block, block, beside)
        moved[k, h].start()

    def turn(k, h):
        block = fetched.at[expert_at[k], :, cols(flip(s, 2), h)]
        crossed[k, h].wait_recv()
        turned[k, h] = remote_to(block, block, beside)
        turned[k, h].start()

    def compute(k):
        e = expert_at[k]
        if k < half:
            for d in moved_s[k]:
                d.wait_recv()
        else:
            for h in range(2):
                moved[k, h].wait_recv()
                turned[k, h].wait_recv()
        back = lax.dot_general(
            fetched[e], down[...], (((1,), (1,)), ((), ())), preferred_element_type=jnp.float32
        )
        gate_pre = pre_pad[e, :, :hidden_part].astype(jnp.float32)
        up_pre = pre_pad[e, :, hidden_part:].astype(jnp.float32)
        sigmoid_gate = jax.nn.sigmoid(gate_pre)
        activated = gate_pre * sigmoid_gate
        hidden = (activated * up_pre).astype(jnp.bfloat16)
        value = jnp.sum(hidden.astype(jnp.float32) * back, axis=1, keepdims=True)
        here = place1[e].astype(jnp.float32) > 0.5
        score_acc[...] += jnp.sum(jnp.where(here, value, 0.0), axis=0, keepdims=True)
        scaled = weight[e] * back
        d_gate = scaled * up_pre * sigmoid_gate * (1.0 + gate_pre * (1.0 - sigmoid_gate))
        both[:, :hidden_part] = d_gate.astype(jnp.bfloat16)
        both[:, hidden_part:] = (scaled * activated).astype(jnp.bfloat16)

        @pl.loop(0, mixing.shape[0] // 512)
        def _(i):
            tile = columns(i, 512)
            part[e, :, tile] = lax.dot_general(
                both[...],
                mixing[tile, :],
                (((1,), (1,)), ((), ())),
                preferred_element_type=jnp.float32,
            ).astype(jnp.bfloat16)

        p = e % half
        if k < half:
            pairs[k] = [
                remote_to(
                    part.at[e, :, columns(2 * q + 1 - c, width)],
                    near_s.at[p, :, pl.ds(q * width, width)],
                    beside,
                )
                for q in range(2)
            ]
        else:
            pairs[k] = [
                remote_to(part.at[e, :, columns(flip(s, bits), width)], near.at[p, i], beside)
                for i, bits in enumerate((3, 1))
            ]
        for d in pairs[k]:
            d.start()

    def gives(k):
        e = expert_at[k]
        p = e % half
        if k:
            for q in range(2):
                sends_s[k, q].wait_send()
        for q in range(2):
            pairs[k][q].wait_recv()
            here = pl.ds(q * width, width)
            value = part[e, :, columns(2 * q + c, width)].astype(jnp.float32)
            value = (value + near_s[p, :, here].astype(jnp.float32)).astype(jnp.bfloat16)
            if k:
                out_s[k, :, here] = value
            else:
                arrived_s[pg, :, here] = value
        if k:
            last[k] = remote_to(out_s.at[k], arrived_s.at[pg], (e, s))
            last[k].start()

    def hand(k, h):
        e = expert_at[k]
        p = e % half
        if once("pair", k, 0):
            pairs[k][0].wait_recv()
        sends[k, h].wait_send()
        value = part[e, :, cols(flip(s, 2), h)].astype(jnp.float32)
        value = value + near[p, 0, :, halves[h]].astype(jnp.float32)
        out_x[k - half, :, halves[h]] = value.astype(jnp.bfloat16)
        middle[k, h] = remote_to(
            out_x.at[k - half, :, halves[h]], far.at[p, :, halves[h]], across
        )
        middle[k, h].start()

    def give(k, h):
        e = expert_at[k]
        p = e % half
        if once("pair", k, 1):
            pairs[k][1].wait_recv()
        middle[k, h].wait_recv()
        value = part[e, :, cols(s, h)].astype(jnp.float32)
        value = value + near[p, 1, :, halves[h]].astype(jnp.float32)
        value = value + far[p, :, halves[h]].astype(jnp.float32)
        sum2[p, :, halves[h]] = value.astype(jnp.bfloat16)
        last[k, h] = remote_to(
            sum2.at[p, :, halves[h]], arrived_x.at[pg, :, halves[h]], (e, s)
        )
        last[k, h].start()

    def score():
        for j in range(1, 4):
            ends.append(remote_to(score_acc, score_out.at[s], (g, seq_at[j])))
            ends[-1].start()
        ends.append(local_copy(score_acc, score_out.at[s]))
        ends[-1].start()

    def token_block(j):
        return pl.ds(pl.multiple_of(seq_at[j] * own_tok, own_tok), own_tok)

    def finish_s():
        for j in range(1, half):
            last[j].wait_recv()
        for q in range(2):
            terms = arrived_s[:, :, q * width : (q + 1) * width].reshape(half * rows, width)
            group[q] = jnp.dot(
                take_t[hg], terms, preferred_element_type=jnp.float32
            ).astype(jnp.bfloat16)
            for j in (2, 3, 1, 0):
                src = group.at[q, token_block(j)]
                dst = same_out.at[y, :, columns(2 * q + c, width)]
                ends.append(remote_to(src, dst, (g, seq_at[j])) if j else local_copy(src, dst))
                ends[-1].start()

    def finish_x(h):
        for j in range(half, n_exp):
            last[j, h].wait_recv()
        terms = arrived_x[:, :, halves[h]].reshape(half * rows, hw)
        acc_x[:, halves[h]] = jnp.dot(
            take_t[1 - hg], terms, preferred_element_type=jnp.float32
        ).astype(jnp.bfloat16)
        for j in (2, 3, 1, 0):
            src = acc_x.at[token_block(j), halves[h]]
            dst = cross_out.at[:, cols(s, h)]
            ends.append(remote_to(src, dst, (g, seq_at[j])) if j else local_copy(src, dst))
            ends[-1].start()

    steps = {
        "csend": csend, "ssend": ssend, "mix": mix, "place": place, "taket": taket, "ready": ready,
        "fwd": fwd, "spread": spread, "turn": turn, "compute": compute, "gives": gives,
        "hand": hand, "give": give, "score": score, "finish_s": finish_s, "finish_x": finish_x,
    }
    for step, numbers in plan():
        steps[step](*numbers)
    for d in id_sends + second:
        d.wait_send()
    for group_of in (first, crossed, moved, turned, middle, last):
        for d in group_of.values():
            d.wait_send()
    for k in range(n_exp):
        for d in pairs[k] + moved_s.get(k, []):
            d.wait_send()
    for d in ends:
        d.wait()


def layer(n_exp, out_grad, chosen, scores, pre, mixing, down):
    own_tok, model_width = out_grad.shape
    capacity = chosen.shape[1]
    width = model_width // 4
    group_tok = own_tok * 4
    rows = 9 * capacity // (8 * n_exp)
    half = n_exp // 2
    hidden2 = 2 * mixing.shape[2]
    step_rows = 512
    kind = out_grad.dtype
    dma = pltpu.SemaphoreType.DMA
    f32 = jnp.float32

    def v(*shape, dtype=kind):
        return pltpu.VMEM(shape, dtype)

    total = 17 * n_exp + 40
    return pl.pallas_call(
        functools.partial(layer_kernel, n_exp, group_tok),
        out_shape=(
            jax.ShapeDtypeStruct((2, own_tok, model_width), kind),
            jax.ShapeDtypeStruct((own_tok, model_width), kind),
            jax.ShapeDtypeStruct((4, 1, capacity), f32),
        ),
        in_specs=[ANY, VMEM, VMEM, ANY, ANY, ANY],
        out_specs=(ANY, ANY, VMEM),
        scratch_shapes=[
            v(n_exp, 1, capacity, dtype=jnp.int32),
            v(2, group_tok, width),
            v(3, n_exp, capacity, dtype=f32),
            v(n_exp, rows, capacity),
            v(n_exp, rows, 1, dtype=f32),
            v(n_exp, rows, group_tok),
            v(2, group_tok, half * rows),
            v(n_exp, rows, 1, dtype=f32),
            v(capacity, hidden2),
            v(n_exp, rows, hidden2),
            v(model_width, hidden2),
            v(hidden2 // 2, model_width),
            v(2, step_rows, 2, hidden2 // 2),
            v(n_exp, rows, model_width),
            v(rows, hidden2),
            v(n_exp, rows, model_width),
            v(half, rows, 2 * width),
            v(half, rows, width),
            v(half, rows, 2 * width),
            v(half, 2, rows, width),
            v(half, rows, width),
            v(half, rows, width),
            v(half, rows, 2 * width),
            v(half, rows, width),
            v(group_tok, width),
            v(1, capacity, dtype=f32),
            dma((20,)),
            dma((total,)),
            dma((total,)),
        ],
        compiler_params=pltpu.CompilerParams(
            collective_id=4, has_side_effects=True, vmem_limit_bytes=60 * 2**20
        ),
    )(out_grad, chosen, scores, pre, mixing, down)


def regroup_kernel(
    n_seq, totals, score, out, score_sum, scores, send, recv, send_s, recv_s, local
):
    g, s = lax.axis_index("exp"), lax.axis_index("seq")
    width = totals.shape[2]
    own = columns(s, width)
    greet([(g, flip(s, k)) for k in range(1, n_seq)])
    copies = []
    for k in range(n_seq - 1, 0, -1):
        t = flip(s, k)
        copies.append(remote(totals.at[t], out.at[:, own], send.at[k], recv.at[k], (g, t)))
        copies[-1].start()
        copies.append(remote(score, scores.at[s], send_s.at[k], recv_s.at[k], (g, t)))
        copies[-1].start()
    mine = pltpu.make_async_copy(totals.at[s], out.at[:, own], local)
    mine.start()
    scores[s] = score[...]
    for c in copies:
        c.wait()
    value = scores[0]
    for k in range(1, n_seq):
        value = value + scores[k]
    score_sum[...] = value
    mine.wait()


def regroup(n_seq, totals, score):
    rows, width = totals.shape[1:]
    dma = pltpu.SemaphoreType.DMA
    return pl.pallas_call(
        functools.partial(regroup_kernel, n_seq),
        out_shape=(
            jax.ShapeDtypeStruct((rows, n_seq * width), totals.dtype),
            jax.ShapeDtypeStruct(score.shape, score.dtype),
        ),
        in_specs=[VMEM, VMEM],
        out_specs=(VMEM, VMEM),
        scratch_shapes=[pltpu.VMEM((n_seq,) + score.shape, score.dtype)]
        + [dma((n_seq,))] * 4
        + [dma],
        compiler_params=pltpu.CompilerParams(collective_id=3, has_side_effects=True),
    )(totals, score)


def counts(hits):
    length = hits.shape[1]
    at = jnp.arange(length, dtype=jnp.int32)
    upper = (at[:, None] <= at[None, :]).astype(jnp.bfloat16)
    total = jnp.dot(hits.astype(jnp.bfloat16), upper, preferred_element_type=jnp.float32)
    return total.astype(jnp.int32)


def local(out_grad, chosen, scores, saved_pre, gate_up, down):
    n_exp = lax.axis_size("exp")
    n_seq = lax.axis_size("seq")
    capacity = chosen.shape[1]
    slot_most = 9 * capacity // (8 * n_exp)
    tok_count, model_width = out_grad.shape
    width = model_width // n_seq
    group_tok = tok_count * n_seq
    pad_rows = n_exp * slot_most
    hidden_part = gate_up.shape[3]
    group_index = lax.axis_index("exp")

    if slot_most % 16 == 0 and n_exp == 8 and n_seq == 4:
        same, cross, score_parts = layer(
            n_exp,
            out_grad,
            chosen,
            scores,
            saved_pre[0],
            gate_up[0],
            down[0],
        )
        value = same[0].astype(jnp.float32) + same[1].astype(jnp.float32)
        value = (value + cross.astype(jnp.float32)).astype(jnp.bfloat16)
        return value, jnp.sum(score_parts, axis=0)

    own_ids = chosen[0]
    owner_group = own_ids // group_tok
    owner_hits = (owner_group[None, :] == jnp.arange(n_exp, dtype=jnp.int32)[:, None]).astype(
        jnp.int32
    )
    slot_order = jnp.sum(counts(owner_hits) * owner_hits, axis=0) - 1
    position = owner_group * slot_most + slot_order
    place = position[None, :] == jnp.arange(pad_rows, dtype=jnp.int32)[:, None]
    weight_padded = jnp.sum(jnp.where(place, scores[0][None, :], 0.0), axis=1)
    place_one = place.astype(jnp.bfloat16)

    def padded(x):
        return jnp.dot(place_one, x, preferred_element_type=jnp.float32)

    gate_pre = padded(saved_pre[0, :, 0])
    up_pre = padded(saved_pre[0, :, 1])
    mixing = gate_up[0].reshape(model_width, 2 * hidden_part)

    ids, group = exchange(n_exp, n_seq, chosen.reshape(capacity // 128, 128), out_grad)
    local_ids = ids.reshape(n_exp, capacity) - group_index * group_tok
    inside = (local_ids >= 0) & (local_ids < group_tok)
    slot_rank = counts(inside) - 1
    slot_ids = jnp.arange(slot_most, dtype=jnp.int32)
    picked = inside[:, None, :] & (slot_rank[:, None, :] == slot_ids[None, :, None])
    source = jnp.sum(jnp.where(picked, local_ids[:, None, :] + 1, 0), axis=2).reshape(pad_rows) - 1
    tokens = jnp.arange(group_tok, dtype=jnp.int32)
    take = (source[:, None] == tokens[None, :]).astype(jnp.bfloat16)
    outgoing = jnp.dot(
        take, group.reshape(group_tok, width), preferred_element_type=jnp.float32
    ).astype(jnp.bfloat16)
    outgoing = outgoing.reshape(n_exp, slot_most, width)
    fetched = dispatch(n_exp, n_seq, outgoing)
    fetched = fetched.reshape(pad_rows, model_width)

    back_grad = lax.dot_general(
        fetched, down[0], (((1,), (1,)), ((), ())), preferred_element_type=jnp.float32
    )
    sigmoid_gate = jax.nn.sigmoid(gate_pre)
    activated = gate_pre * sigmoid_gate
    hidden = (activated * up_pre).astype(jnp.bfloat16)
    hidden = lax.optimization_barrier(hidden)
    score_part = jnp.sum(hidden.astype(jnp.float32) * back_grad, axis=1)
    scaled = weight_padded[:, None] * back_grad
    d_gate = scaled * up_pre * sigmoid_gate * (1.0 + gate_pre * (1.0 - sigmoid_gate))
    d_up = scaled * activated
    d_both = jnp.concatenate([d_gate, d_up], axis=1).astype(jnp.bfloat16)
    partial_value = lax.dot_general(
        d_both, mixing, (((1,), (1,)), ((), ())), preferred_element_type=jnp.float32
    ).astype(jnp.bfloat16)
    arrived = combine(n_exp, n_seq, partial_value.reshape(n_exp, slot_most, model_width))
    score_slots = jnp.sum(jnp.where(place, score_part[:, None], 0.0), axis=0)
    totals = lax.dot_general(
        take,
        arrived.reshape(pad_rows, width),
        (((0,), (0,)), ((), ())),
        preferred_element_type=jnp.float32,
    ).astype(jnp.bfloat16)
    summed, score_grad = regroup(
        n_seq,
        totals.reshape(n_seq, tok_count, width),
        score_slots.reshape(capacity // 128, 128),
    )
    return (summed, score_grad.reshape(1, capacity))


def solution(mesh):
    return jax.shard_map(
        local,
        mesh=mesh,
        in_specs=(
            P(("exp", "seq"), None),
            P("exp", None),
            P("exp", None),
            P("exp", None, None, "seq"),
            P("exp", None, None, "seq"),
            P("exp", "seq", None),
        ),
        out_specs=(P(("exp", "seq"), None), P("exp", None)),
        check_vma=False,
    )
```

```python
import functools

import jax
import jax.numpy as jnp
from jax import lax
from jax.experimental import pallas as pl
from jax.experimental.pallas import tpu as pltpu
from jax.sharding import PartitionSpec as P

MESH = pl.DeviceIdType.MESH
ANY = pl.BlockSpec(memory_space=pl.ANY)
VMEM = pl.BlockSpec(memory_space=pltpu.VMEM)


def flip(index, bits):
    out, step = index, 1
    while bits >= step:
        if bits & step:
            out = out + step * (1 - 2 * ((index // step) % 2))
        step *= 2
    return out


def greet(peers):
    barrier = pltpu.get_barrier_semaphore()
    for p in peers:
        pl.semaphore_signal(barrier, inc=1, device_id=p, device_id_type=MESH)
    pl.semaphore_wait(barrier, len(peers))


def remote(src, dst, send, recv, to):
    return pltpu.make_async_remote_copy(
        src_ref=src, dst_ref=dst, send_sem=send, recv_sem=recv, device_id=to, device_id_type=MESH
    )


def columns(quarter, width):
    return pl.ds(pl.multiple_of(quarter * width, 128), width)


def exchange_kernel(n_exp, n_seq, chosen, grad, ids, group, send_i, recv_i, send_g, recv_g, local):
    g, s = lax.axis_index("exp"), lax.axis_index("seq")
    width = grad.shape[1] // n_seq
    greet([(flip(g, k), s) for k in range(1, n_exp)] + [(g, flip(s, k)) for k in range(1, n_seq)])
    copies = []
    for k in range(1, n_exp):
        copies.append(remote(chosen, ids.at[g], send_i.at[k], recv_i.at[k], (flip(g, k), s)))
        copies[-1].start()
    for k in range(n_seq - 1, 0, -1):
        t = flip(s, k)
        copies.append(
            remote(grad.at[:, columns(t, width)], group.at[s], send_g.at[k], recv_g.at[k], (g, t))
        )
        copies[-1].start()
    own_ids = pltpu.make_async_copy(chosen, ids.at[g], local.at[0])
    own_grad = pltpu.make_async_copy(grad.at[:, columns(s, width)], group.at[s], local.at[1])
    own_ids.start()
    own_grad.start()
    for c in copies:
        c.wait()
    own_ids.wait()
    own_grad.wait()


def exchange(n_exp, n_seq, chosen, grad):
    rows, width = grad.shape[0], grad.shape[1] // n_seq
    dma = pltpu.SemaphoreType.DMA
    return pl.pallas_call(
        functools.partial(exchange_kernel, n_exp, n_seq),
        out_shape=(
            jax.ShapeDtypeStruct((n_exp,) + chosen.shape, chosen.dtype),
            jax.ShapeDtypeStruct((n_seq, rows, width), grad.dtype),
        ),
        in_specs=[VMEM, VMEM],
        out_specs=(VMEM, VMEM),
        scratch_shapes=[dma((n_exp,)), dma((n_exp,)), dma((n_seq,)), dma((n_seq,)), dma((2,))],
        compiler_params=pltpu.CompilerParams(collective_id=0, has_side_effects=True),
    )(chosen, grad)


def dispatch_kernel(n_exp, out, fetched, s0, r0, sa, ra, sb, rb, sc, rc, local):
    g, s = lax.axis_index("exp"), lax.axis_index("seq")
    width = out.shape[2]
    across, beside = (g, flip(s, 2)), (g, flip(s, 1))
    own, theirs = columns(s, width), columns(flip(s, 2), width)
    greet([(flip(g, k), s) for k in range(1, n_exp)] + [across, beside])
    first = pltpu.make_async_copy(out.at[g], fetched.at[g, :, own], local)
    first.start()
    half = n_exp // 2
    order = []
    for k in range(half):
        order.append(half + k)
        if k:
            order.append(k)
    sends = {}
    for k in order:
        e = flip(g, k)
        sends[k] = remote(out.at[e], fetched.at[g, :, own], s0.at[k], r0.at[k], (e, s))
        sends[k].start()
    crossed, done = [], []
    for k in range(n_exp):
        block = fetched.at[flip(g, k)]
        if k:
            sends[k].wait_recv()
        else:
            first.wait()
        c = remote(block.at[:, own], block.at[:, own], sa.at[k], ra.at[k], across)
        c.start()
        crossed.append(c)
        d = remote(block.at[:, own], block.at[:, own], sb.at[k], rb.at[k], beside)
        d.start()
        done.append(d)
    for k in range(n_exp):
        block = fetched.at[flip(g, k)]
        crossed[k].wait_recv()
        d = remote(block.at[:, theirs], block.at[:, theirs], sc.at[k], rc.at[k], beside)
        d.start()
        done.append(d)
    for k in order:
        sends[k].wait_send()
    for c in crossed:
        c.wait_send()
    for d in done:
        d.wait()


def dispatch(n_exp, n_seq, out):
    rows, width = out.shape[1:]
    dma = pltpu.SemaphoreType.DMA
    return pl.pallas_call(
        functools.partial(dispatch_kernel, n_exp),
        out_shape=jax.ShapeDtypeStruct((n_exp, rows, n_seq * width), out.dtype),
        in_specs=[ANY],
        out_specs=ANY,
        scratch_shapes=[dma((n_exp,))] * 8 + [dma],
        compiler_params=pltpu.CompilerParams(collective_id=1, has_side_effects=True),
    )(out)


def combine_kernel(n_exp, part, arrived, near, sum1, far, sum2, s1, r1, s2, r2, s3, r3, local):
    g, s = lax.axis_index("exp"), lax.axis_index("seq")
    width = arrived.shape[2]
    across, beside = (g, flip(s, 2)), (g, flip(s, 1))
    own, theirs = columns(s, width), columns(flip(s, 2), width)
    greet([(flip(g, k), s) for k in range(1, n_exp)] + [across, beside])
    half = n_exp // 2
    order = list(range(half, n_exp)) + list(range(1, half)) + [0]
    pairs = {}
    for k in order:
        e = flip(g, k)
        pairs[k] = [
            remote(
                part.at[e, :, columns(flip(s, bits), width)],
                near.at[e, i],
                s1.at[k, i],
                r1.at[k, i],
                beside,
            )
            for i, bits in enumerate((3, 1))
        ]
        for c in pairs[k]:
            c.start()
    middle, last = {}, {}
    for k in order:
        e = flip(g, k)
        pairs[k][0].wait_recv()
        both = part[e, :, theirs].astype(jnp.float32) + near[e, 0].astype(jnp.float32)
        sum1[e] = both.astype(jnp.bfloat16)
        middle[k] = remote(sum1.at[e], far.at[e], s2.at[k], r2.at[k], across)
        middle[k].start()
    for k in order:
        e = flip(g, k)
        pairs[k][1].wait_recv()
        middle[k].wait_recv()
        total = part[e, :, own].astype(jnp.float32) + near[e, 1].astype(jnp.float32)
        total = total + far[e].astype(jnp.float32)
        sum2[e] = total.astype(jnp.bfloat16)
        if k:
            last[k] = remote(sum2.at[e], arrived.at[g], s3.at[k], r3.at[k], (e, s))
        else:
            last[k] = pltpu.make_async_copy(sum2.at[e], arrived.at[g], local)
        last[k].start()
    for k in order:
        for c in pairs[k]:
            c.wait_send()
        middle[k].wait_send()
        last[k].wait()


def combine(n_exp, n_seq, part):
    rows, width = part.shape[1], part.shape[2] // n_seq
    dma = pltpu.SemaphoreType.DMA
    block = pltpu.VMEM((n_exp, rows, width), part.dtype)
    return pl.pallas_call(
        functools.partial(combine_kernel, n_exp),
        out_shape=jax.ShapeDtypeStruct((n_exp, rows, width), part.dtype),
        in_specs=[VMEM],
        out_specs=VMEM,
        scratch_shapes=[pltpu.VMEM((n_exp, 2, rows, width), part.dtype), block, block, block]
        + [dma((n_exp, 2))] * 2
        + [dma((n_exp,))] * 4
        + [dma],
        compiler_params=pltpu.CompilerParams(
            collective_id=2, has_side_effects=True, vmem_limit_bytes=48 * 2**20
        ),
    )(part)


def running_count(hits):
    rows, length = hits.shape
    ahead = lax.broadcasted_iota(jnp.int32, (128, 128), 0)
    here = lax.broadcasted_iota(jnp.int32, (128, 128), 1)
    upper = (ahead <= here).astype(jnp.float32).astype(jnp.bfloat16)
    hits = hits.astype(jnp.float32)
    before = jnp.zeros((rows, 1), jnp.float32)
    out = []
    for j in range(length // 128):
        block = hits[:, j * 128 : (j + 1) * 128]
        count = jnp.dot(block.astype(jnp.bfloat16), upper, preferred_element_type=jnp.float32)
        out.append(count + before)
        before = before + jnp.sum(block, axis=1, keepdims=True)
    return jnp.concatenate(out, axis=1)


ORDER = [
    "mix 0", "csend 5 0", "taket", "mix 1", "csend 5 1", "csend 4 1", "ssend 2 0", "ssend 1 0",
    "csend 4 0", "mix 2", "spread 5 0", "place", "ssend 2 1", "mix 3", "csend 6 0", "mix 4",
    "csend 7 0", "ssend 1 1", "spread 5 1", "ssend 0 0", "ssend 3 1", "csend 7 1", "mix 5",
    "spread 4 1", "mix 6", "fwd 1 0", "fwd 2 0", "turn 5 0", "turn 5 1", "mix 7", "mix 8", "mix 9",
    "fwd 1 1", "ready", "turn 4 1", "fwd 2 1", "spread 4 0", "compute 5", "ssend 3 0", "turn 4 0",
    "fwd 0 0", "compute 2", "spread 6 0", "ssend 0 1", "fwd 0 1", "hand 5 1", "hand 5 0",
    "csend 6 1", "compute 4", "spread 7 0", "turn 6 0", "compute 1", "fwd 3 1", "hand 4 1",
    "spread 7 1", "give 5 0", "fwd 3 0", "gives 2 0", "compute 0", "gives 1 0", "spread 6 1",
    "compute 3", "give 4 1", "gives 0 1", "turn 7 1", "turn 6 1", "give 5 1", "turn 7 0",
    "hand 4 0", "gives 3 0", "compute 6", "compute 7", "hand 6 1", "gives 1 1", "gives 2 1",
    "gives 3 1", "give 4 0", "hand 7 1", "gives 0 0", "hand 7 0", "hand 6 0", "score", "give 6 1",
    "finish_s 0", "give 7 1", "give 6 0", "finish_s 1", "give 7 0", "finish_x 1", "finish_x 0",
]


def plan():
    for step in ORDER:
        name, *numbers = step.split()
        yield name, [int(n) for n in numbers]


def layer_kernel(
    n_exp, group_tok, grad, chosen, scores, pre_in, mixing_in, down_in, same_out, cross_out, score_out,
    ids, group, rank, place1, weight, take, take_t, spot, pre, pre_pad, mixing, down, raw,
    fetched, both, part, out_s, out_x, near_s, near, far, sum2, arrived_s, arrived_x, acc_x,
    score_acc, dma, dma_s, dma_r,
):
    g, s = lax.axis_index("exp"), lax.axis_index("seq")
    half = n_exp // 2
    rows = take.shape[1]
    width = group.shape[2]
    own_tok = group_tok // 4
    hw = width // 2
    hidden_part = down.shape[0]
    y, c = s // 2, s % 2
    hg, pg = g // half, g % half
    across, beside = (g, flip(s, 2)), (g, flip(s, 1))
    own, theirs = columns(s, width), columns(flip(s, 2), width)
    expert_at = [flip(g, k) for k in range(n_exp)]
    seq_at = [flip(s, k) for k in range(4)]
    count = {"n": 0, "local": 0}
    halves = [pl.ds(h * hw, hw) for h in range(2)]

    def cols(quarter, h):
        return pl.ds(pl.multiple_of(quarter * width + h * hw, 128), hw)

    def remote_to(src, dst, to):
        n = count["n"]
        count["n"] = n + 1
        return remote(src, dst, dma_s.at[n], dma_r.at[n], to)

    def local_copy(src, dst):
        n = count["local"]
        count["local"] = n + 1
        return pltpu.make_async_copy(src, dst, dma.at[n])

    get_down = local_copy(down_in, down)
    step_rows = raw.shape[1]
    raw_parts = [(src, dst, i) for src, dst in ((pre_in, pre), (mixing_in, mixing))
                 for i in range(dst.shape[0] // step_rows)]
    raw_copies = [
        local_copy(src.at[pl.ds(i * step_rows, step_rows)], raw.at[n % 2])
        for n, (src, _, i) in enumerate(raw_parts)
    ]
    greet([(e, s) for e in expert_at[1:]] + [(g, t) for t in seq_at[1:]])
    id_sends, first, second = [], {}, []
    side = (y, 1 - y)
    for k in range(1, n_exp):
        id_sends.append(remote_to(chosen, ids.at[g], (expert_at[k], s)))
        id_sends[-1].start()
    mine = pl.ds(pl.multiple_of(s * own_tok, own_tok), own_tok)
    for h in range(2):
        for k in (2, 3, 1):
            t = seq_at[k]
            first[k, h] = remote_to(
                grad.at[:, cols(t, h)], group.at[t // 2, mine, halves[h]], (g, t)
            )
            first[k, h].start()
    for k in (2, 3, 1):
        t = seq_at[k]
        second.append(
            remote_to(grad.at[:, columns(flip(t, 2), width)], group.at[1 - t // 2, mine], (g, t))
        )
        second[-1].start()
    own_copies = [
        local_copy(chosen, ids.at[g]),
        local_copy(grad.at[:, own], group.at[y, mine]),
        local_copy(grad.at[:, theirs], group.at[1 - y, mine]),
    ]
    for d in own_copies:
        d.start()
    get_down.start()
    raw_copies[0].start()

    capacity = chosen.shape[1]
    row = lax.broadcasted_iota(jnp.int32, (n_exp, capacity), 0)
    slot = lax.broadcasted_iota(jnp.int32, (rows, capacity), 0).astype(jnp.float32)

    for d in id_sends:
        d.wait_recv()
    own_copies[0].wait()
    local = jnp.zeros((n_exp, capacity), jnp.int32)
    for e in range(n_exp):
        local = jnp.where(row == e, ids[e], local)
    local = local - g * group_tok
    inside = (local >= 0) & (local < group_tok)
    rank[0] = jnp.where(inside, running_count(inside) - 1.0, -1.0)
    rank[1] = (local + 1).astype(jnp.float32)

    @pl.loop(0, n_exp)
    def _(e):
        picked = rank[0, pl.ds(e, 1), :] == slot
        at = jnp.sum(jnp.where(picked, rank[1, pl.ds(e, 1), :], 0.0), axis=1, keepdims=True) - 1.0
        spot[e] = at
        token = lax.broadcasted_iota(jnp.int32, (rows, group_tok), 1).astype(jnp.float32)
        take[e] = (at == token).astype(jnp.float32).astype(jnp.bfloat16)

    def select(e, q):
        return jnp.dot(take[e], group[q], preferred_element_type=jnp.float32).astype(jnp.bfloat16)

    sends, sends_s, moved_s = {}, {}, {}
    crossed, moved, turned, pairs, middle, last, ends = {}, {}, {}, {}, {}, {}, []
    seen = set()
    score_acc[...] = jnp.zeros_like(score_acc)

    def once(*key):
        new = key not in seen
        seen.add(key)
        return new

    def csend(k, h):
        if once("own"):
            own_copies[1].wait()
        if once("first", h):
            for j in (2, 3, 1):
                first[j, h].wait_recv()
        e = expert_at[k]
        out_x[k - half, :, halves[h]] = jnp.dot(
            take[e], group[y, :, halves[h]], preferred_element_type=jnp.float32
        ).astype(jnp.bfloat16)
        sends[k, h] = remote_to(
            out_x.at[k - half, :, halves[h]], fetched.at[g, :, cols(s, h)], (e, s)
        )
        sends[k, h].start()

    def ssend(k, i):
        if once("own"):
            own_copies[1].wait()
        if i == 0:
            for h in range(2):
                if once("first", h):
                    for j in (2, 3, 1):
                        first[j, h].wait_recv()
        elif once("second"):
            for d in second:
                d.wait_recv()
            own_copies[2].wait()
        e = expert_at[k]
        if k:
            here = pl.ds(i * width, width)
            out_s[k, :, here] = select(e, side[i])
            sends_s[k, i] = remote_to(
                out_s.at[k, :, here], fetched.at[g, :, columns(flip(s, 2 * i), width)], (e, s)
            )
            sends_s[k, i].start()
        else:
            fetched[g, :, columns(flip(s, 2 * i), width)] = select(e, side[i])

    def mix(n):
        if n + 1 < len(raw_copies):
            raw_copies[n + 1].start()
        raw_copies[n].wait()
        _, dst, i = raw_parts[n]
        dst[i * step_rows : (i + 1) * step_rows, :] = raw[n % 2].reshape(
            step_rows, 2 * hidden_part
        )

    def place():
        ids_here = chosen[...]
        low = row * group_tok
        hits = (ids_here >= low) & (ids_here < low + group_tok)
        rank[2] = jnp.where(hits, running_count(hits) - 1.0, -1.0)

        @pl.loop(0, n_exp)
        def _(e):
            picked = rank[2, pl.ds(e, 1), :] == slot
            place1[e] = picked.astype(jnp.float32).astype(jnp.bfloat16)
            weight[e] = jnp.sum(jnp.where(picked, scores[...], 0.0), axis=1, keepdims=True)
            pre_pad[e] = jnp.dot(
                place1[e], pre[...], preferred_element_type=jnp.float32
            ).astype(jnp.bfloat16)

    def taket():
        @pl.loop(0, 2)
        def _(h):
            at = spot[pl.ds(h * half, half)].reshape(half * rows, 1)
            a = lax.broadcasted_iota(jnp.int32, (half * rows, half * rows), 0)
            b = lax.broadcasted_iota(jnp.int32, (half * rows, half * rows), 1)
            flat = jnp.sum(jnp.where(a == b, at, 0.0), axis=0, keepdims=True)
            token = lax.broadcasted_iota(jnp.int32, (group_tok, half * rows), 0)
            token = token.astype(jnp.float32)
            take_t[h] = (token == flat).astype(jnp.float32).astype(jnp.bfloat16)

    def ready():
        get_down.wait()

    def fwd(k, i):
        if k:
            sends_s[k, i].wait_recv()
        block = fetched.at[expert_at[k], :, columns(flip(s, 2 * i), width)]
        moved_s[k, i] = remote_to(block, block, beside)
        moved_s[k, i].start()

    def spread(k, h):
        block = fetched.at[expert_at[k], :, cols(s, h)]
        sends[k, h].wait_recv()
        crossed[k, h] = remote_to(block, block, across)
        crossed[k, h].start()
        moved[k, h] = remote_to(block, block, beside)
        moved[k, h].start()

    def turn(k, h):
        block = fetched.at[expert_at[k], :, cols(flip(s, 2), h)]
        crossed[k, h].wait_recv()
        turned[k, h] = remote_to(block, block, beside)
        turned[k, h].start()

    def compute(k):
        e = expert_at[k]
        if k < half:
            for i in range(2):
                moved_s[k, i].wait_recv()
        else:
            for h in range(2):
                moved[k, h].wait_recv()
                turned[k, h].wait_recv()
        back = lax.dot_general(
            fetched[e], down[...], (((1,), (1,)), ((), ())), preferred_element_type=jnp.float32
        )
        gate_pre = pre_pad[e, :, :hidden_part].astype(jnp.float32)
        up_pre = pre_pad[e, :, hidden_part:].astype(jnp.float32)
        sigmoid_gate = jax.nn.sigmoid(gate_pre)
        activated = gate_pre * sigmoid_gate
        hidden = (activated * up_pre).astype(jnp.bfloat16)
        value = jnp.sum(hidden.astype(jnp.float32) * back, axis=1, keepdims=True)
        here = place1[e].astype(jnp.float32) > 0.5
        score_acc[...] += jnp.sum(jnp.where(here, value, 0.0), axis=0, keepdims=True)
        scaled = weight[e] * back
        d_gate = scaled * up_pre * sigmoid_gate * (1.0 + gate_pre * (1.0 - sigmoid_gate))
        both[:, :hidden_part] = d_gate.astype(jnp.bfloat16)
        both[:, hidden_part:] = (scaled * activated).astype(jnp.bfloat16)

        @pl.loop(0, mixing.shape[0] // 512)
        def _(i):
            tile = columns(i, 512)
            part[e, :, tile] = lax.dot_general(
                both[...],
                mixing[tile, :],
                (((1,), (1,)), ((), ())),
                preferred_element_type=jnp.float32,
            ).astype(jnp.bfloat16)

        p = e % half
        if k < half:
            pairs[k] = [
                remote_to(
                    part.at[e, :, columns(flip(s, 2 * i + 1), width)],
                    near_s.at[p, :, pl.ds(i * width, width)],
                    beside,
                )
                for i in range(2)
            ]
        else:
            pairs[k] = [
                remote_to(part.at[e, :, columns(flip(s, bits), width)], near.at[p, i], beside)
                for i, bits in enumerate((3, 1))
            ]
        for d in pairs[k]:
            d.start()

    def gives(k, i):
        e = expert_at[k]
        p = e % half
        here = pl.ds(i * width, width)
        pairs[k][i].wait_recv()
        value = part[e, :, columns(flip(s, 2 * i), width)].astype(jnp.float32)
        value = (value + near_s[p, :, here].astype(jnp.float32)).astype(jnp.bfloat16)
        if k:
            sends_s[k, i].wait_send()
            out_s[k, :, here] = value
            last[k, i] = remote_to(out_s.at[k, :, here], arrived_s.at[pg, :, here], (e, s))
            last[k, i].start()
        else:
            arrived_s[pg, :, here] = value

    def hand(k, h):
        e = expert_at[k]
        p = e % half
        if once("pair", k, 0):
            pairs[k][0].wait_recv()
        sends[k, h].wait_send()
        value = part[e, :, cols(flip(s, 2), h)].astype(jnp.float32)
        value = value + near[p, 0, :, halves[h]].astype(jnp.float32)
        out_x[k - half, :, halves[h]] = value.astype(jnp.bfloat16)
        middle[k, h] = remote_to(
            out_x.at[k - half, :, halves[h]], far.at[p, :, halves[h]], across
        )
        middle[k, h].start()

    def give(k, h):
        e = expert_at[k]
        p = e % half
        if once("pair", k, 1):
            pairs[k][1].wait_recv()
        middle[k, h].wait_recv()
        value = part[e, :, cols(s, h)].astype(jnp.float32)
        value = value + near[p, 1, :, halves[h]].astype(jnp.float32)
        value = value + far[p, :, halves[h]].astype(jnp.float32)
        sum2[p, :, halves[h]] = value.astype(jnp.bfloat16)
        last[k, h] = remote_to(
            sum2.at[p, :, halves[h]], arrived_x.at[pg, :, halves[h]], (e, s)
        )
        last[k, h].start()

    def score():
        for j in range(1, 4):
            ends.append(remote_to(score_acc, score_out.at[s], (g, seq_at[j])))
            ends[-1].start()
        ends.append(local_copy(score_acc, score_out.at[s]))
        ends[-1].start()

    def token_block(j):
        return pl.ds(pl.multiple_of(seq_at[j] * own_tok, own_tok), own_tok)

    def finish_s(i):
        for j in range(1, half):
            last[j, i].wait_recv()
        terms = arrived_s[:, :, i * width : (i + 1) * width].reshape(half * rows, width)
        group[i] = jnp.dot(
            take_t[hg], terms, preferred_element_type=jnp.float32
        ).astype(jnp.bfloat16)
        for j in (2, 3, 1, 0):
            src = group.at[i, token_block(j)]
            dst = same_out.at[y, :, columns(flip(s, 2 * i), width)]
            ends.append(remote_to(src, dst, (g, seq_at[j])) if j else local_copy(src, dst))
            ends[-1].start()

    def finish_x(h):
        for j in range(half, n_exp):
            last[j, h].wait_recv()
        terms = arrived_x[:, :, halves[h]].reshape(half * rows, hw)
        acc_x[:, halves[h]] = jnp.dot(
            take_t[1 - hg], terms, preferred_element_type=jnp.float32
        ).astype(jnp.bfloat16)
        for j in (2, 3, 1, 0):
            src = acc_x.at[token_block(j), halves[h]]
            dst = cross_out.at[:, cols(s, h)]
            ends.append(remote_to(src, dst, (g, seq_at[j])) if j else local_copy(src, dst))
            ends[-1].start()

    steps = {
        "csend": csend, "ssend": ssend, "mix": mix, "place": place, "taket": taket, "ready": ready,
        "fwd": fwd, "spread": spread, "turn": turn, "compute": compute, "gives": gives,
        "hand": hand, "give": give, "score": score, "finish_s": finish_s, "finish_x": finish_x,
    }
    for step, numbers in plan():
        steps[step](*numbers)
    for d in id_sends + second:
        d.wait_send()
    for group_of in (first, crossed, moved, turned, moved_s, middle, last):
        for d in group_of.values():
            d.wait_send()
    for k in range(n_exp):
        for d in pairs[k]:
            d.wait_send()
    for d in ends:
        d.wait()


def layer(n_exp, out_grad, chosen, scores, pre, mixing, down):
    own_tok, model_width = out_grad.shape
    capacity = chosen.shape[1]
    width = model_width // 4
    group_tok = own_tok * 4
    rows = 9 * capacity // (8 * n_exp)
    half = n_exp // 2
    hidden2 = 2 * mixing.shape[2]
    step_rows = 512
    kind = out_grad.dtype
    dma = pltpu.SemaphoreType.DMA
    f32 = jnp.float32

    def v(*shape, dtype=kind):
        return pltpu.VMEM(shape, dtype)

    total = 17 * n_exp + 40
    return pl.pallas_call(
        functools.partial(layer_kernel, n_exp, group_tok),
        out_shape=(
            jax.ShapeDtypeStruct((2, own_tok, model_width), kind),
            jax.ShapeDtypeStruct((own_tok, model_width), kind),
            jax.ShapeDtypeStruct((4, 1, capacity), f32),
        ),
        in_specs=[ANY, VMEM, VMEM, ANY, ANY, ANY],
        out_specs=(ANY, ANY, VMEM),
        scratch_shapes=[
            v(n_exp, 1, capacity, dtype=jnp.int32),
            v(2, group_tok, width),
            v(3, n_exp, capacity, dtype=f32),
            v(n_exp, rows, capacity),
            v(n_exp, rows, 1, dtype=f32),
            v(n_exp, rows, group_tok),
            v(2, group_tok, half * rows),
            v(n_exp, rows, 1, dtype=f32),
            v(capacity, hidden2),
            v(n_exp, rows, hidden2),
            v(model_width, hidden2),
            v(hidden2 // 2, model_width),
            v(2, step_rows, 2, hidden2 // 2),
            v(n_exp, rows, model_width),
            v(rows, hidden2),
            v(n_exp, rows, model_width),
            v(half, rows, 2 * width),
            v(half, rows, width),
            v(half, rows, 2 * width),
            v(half, 2, rows, width),
            v(half, rows, width),
            v(half, rows, width),
            v(half, rows, 2 * width),
            v(half, rows, width),
            v(group_tok, width),
            v(1, capacity, dtype=f32),
            dma((20,)),
            dma((total,)),
            dma((total,)),
        ],
        compiler_params=pltpu.CompilerParams(
            collective_id=4, has_side_effects=True, vmem_limit_bytes=60 * 2**20
        ),
    )(out_grad, chosen, scores, pre, mixing, down)


def regroup_kernel(
    n_seq, totals, score, out, score_sum, scores, send, recv, send_s, recv_s, local
):
    g, s = lax.axis_index("exp"), lax.axis_index("seq")
    width = totals.shape[2]
    own = columns(s, width)
    greet([(g, flip(s, k)) for k in range(1, n_seq)])
    copies = []
    for k in range(n_seq - 1, 0, -1):
        t = flip(s, k)
        copies.append(remote(totals.at[t], out.at[:, own], send.at[k], recv.at[k], (g, t)))
        copies[-1].start()
        copies.append(remote(score, scores.at[s], send_s.at[k], recv_s.at[k], (g, t)))
        copies[-1].start()
    mine = pltpu.make_async_copy(totals.at[s], out.at[:, own], local)
    mine.start()
    scores[s] = score[...]
    for c in copies:
        c.wait()
    value = scores[0]
    for k in range(1, n_seq):
        value = value + scores[k]
    score_sum[...] = value
    mine.wait()


def regroup(n_seq, totals, score):
    rows, width = totals.shape[1:]
    dma = pltpu.SemaphoreType.DMA
    return pl.pallas_call(
        functools.partial(regroup_kernel, n_seq),
        out_shape=(
            jax.ShapeDtypeStruct((rows, n_seq * width), totals.dtype),
            jax.ShapeDtypeStruct(score.shape, score.dtype),
        ),
        in_specs=[VMEM, VMEM],
        out_specs=(VMEM, VMEM),
        scratch_shapes=[pltpu.VMEM((n_seq,) + score.shape, score.dtype)]
        + [dma((n_seq,))] * 4
        + [dma],
        compiler_params=pltpu.CompilerParams(collective_id=3, has_side_effects=True),
    )(totals, score)


def counts(hits):
    length = hits.shape[1]
    at = jnp.arange(length, dtype=jnp.int32)
    upper = (at[:, None] <= at[None, :]).astype(jnp.bfloat16)
    total = jnp.dot(hits.astype(jnp.bfloat16), upper, preferred_element_type=jnp.float32)
    return total.astype(jnp.int32)


def local(out_grad, chosen, scores, saved_pre, gate_up, down):
    n_exp = lax.axis_size("exp")
    n_seq = lax.axis_size("seq")
    capacity = chosen.shape[1]
    slot_most = 9 * capacity // (8 * n_exp)
    tok_count, model_width = out_grad.shape
    width = model_width // n_seq
    group_tok = tok_count * n_seq
    pad_rows = n_exp * slot_most
    hidden_part = gate_up.shape[3]
    group_index = lax.axis_index("exp")

    if slot_most % 16 == 0 and n_exp == 8 and n_seq == 4:
        same, cross, score_parts = layer(
            n_exp,
            out_grad,
            chosen,
            scores,
            saved_pre[0],
            gate_up[0],
            down[0],
        )
        value = same[0].astype(jnp.float32) + same[1].astype(jnp.float32)
        value = (value + cross.astype(jnp.float32)).astype(jnp.bfloat16)
        return value, jnp.sum(score_parts, axis=0)

    own_ids = chosen[0]
    owner_group = own_ids // group_tok
    owner_hits = (owner_group[None, :] == jnp.arange(n_exp, dtype=jnp.int32)[:, None]).astype(
        jnp.int32
    )
    slot_order = jnp.sum(counts(owner_hits) * owner_hits, axis=0) - 1
    position = owner_group * slot_most + slot_order
    place = position[None, :] == jnp.arange(pad_rows, dtype=jnp.int32)[:, None]
    weight_padded = jnp.sum(jnp.where(place, scores[0][None, :], 0.0), axis=1)
    place_one = place.astype(jnp.bfloat16)

    def padded(x):
        return jnp.dot(place_one, x, preferred_element_type=jnp.float32)

    gate_pre = padded(saved_pre[0, :, 0])
    up_pre = padded(saved_pre[0, :, 1])
    mixing = gate_up[0].reshape(model_width, 2 * hidden_part)

    ids, group = exchange(n_exp, n_seq, chosen.reshape(capacity // 128, 128), out_grad)
    local_ids = ids.reshape(n_exp, capacity) - group_index * group_tok
    inside = (local_ids >= 0) & (local_ids < group_tok)
    slot_rank = counts(inside) - 1
    slot_ids = jnp.arange(slot_most, dtype=jnp.int32)
    picked = inside[:, None, :] & (slot_rank[:, None, :] == slot_ids[None, :, None])
    source = jnp.sum(jnp.where(picked, local_ids[:, None, :] + 1, 0), axis=2).reshape(pad_rows) - 1
    tokens = jnp.arange(group_tok, dtype=jnp.int32)
    take = (source[:, None] == tokens[None, :]).astype(jnp.bfloat16)
    outgoing = jnp.dot(
        take, group.reshape(group_tok, width), preferred_element_type=jnp.float32
    ).astype(jnp.bfloat16)
    outgoing = outgoing.reshape(n_exp, slot_most, width)
    fetched = dispatch(n_exp, n_seq, outgoing)
    fetched = fetched.reshape(pad_rows, model_width)

    back_grad = lax.dot_general(
        fetched, down[0], (((1,), (1,)), ((), ())), preferred_element_type=jnp.float32
    )
    sigmoid_gate = jax.nn.sigmoid(gate_pre)
    activated = gate_pre * sigmoid_gate
    hidden = (activated * up_pre).astype(jnp.bfloat16)
    hidden = lax.optimization_barrier(hidden)
    score_part = jnp.sum(hidden.astype(jnp.float32) * back_grad, axis=1)
    scaled = weight_padded[:, None] * back_grad
    d_gate = scaled * up_pre * sigmoid_gate * (1.0 + gate_pre * (1.0 - sigmoid_gate))
    d_up = scaled * activated
    d_both = jnp.concatenate([d_gate, d_up], axis=1).astype(jnp.bfloat16)
    partial_value = lax.dot_general(
        d_both, mixing, (((1,), (1,)), ((), ())), preferred_element_type=jnp.float32
    ).astype(jnp.bfloat16)
    arrived = combine(n_exp, n_seq, partial_value.reshape(n_exp, slot_most, model_width))
    score_slots = jnp.sum(jnp.where(place, score_part[:, None], 0.0), axis=0)
    totals = lax.dot_general(
        take,
        arrived.reshape(pad_rows, width),
        (((0,), (0,)), ((), ())),
        preferred_element_type=jnp.float32,
    ).astype(jnp.bfloat16)
    summed, score_grad = regroup(
        n_seq,
        totals.reshape(n_seq, tok_count, width),
        score_slots.reshape(capacity // 128, 128),
    )
    return (summed, score_grad.reshape(1, capacity))


def solution(mesh):
    return jax.shard_map(
        local,
        mesh=mesh,
        in_specs=(
            P(("exp", "seq"), None),
            P("exp", None),
            P("exp", None),
            P("exp", None, None, "seq"),
            P("exp", None, None, "seq"),
            P("exp", "seq", None),
        ),
        out_specs=(P(("exp", "seq"), None), P("exp", None)),
        check_vma=False,
    )
```

```python
import functools

import jax
import jax.numpy as jnp
from jax import lax
from jax.experimental import pallas as pl
from jax.experimental.pallas import tpu as pltpu
from jax.sharding import PartitionSpec as P

MESH = pl.DeviceIdType.MESH
PIECES = 2
ANY = pl.BlockSpec(memory_space=pl.ANY)
VMEM = pl.BlockSpec(memory_space=pltpu.VMEM)


def flip(index, bits):
    out, step = index, 1
    while bits >= step:
        if bits & step:
            out = out + step * (1 - 2 * ((index // step) % 2))
        step *= 2
    return out


def greet(peers):
    barrier = pltpu.get_barrier_semaphore()
    for p in peers:
        pl.semaphore_signal(barrier, inc=1, device_id=p, device_id_type=MESH)
    pl.semaphore_wait(barrier, len(peers))


def remote(src, dst, send, recv, to):
    return pltpu.make_async_remote_copy(
        src_ref=src, dst_ref=dst, send_sem=send, recv_sem=recv, device_id=to, device_id_type=MESH
    )


def columns(quarter, width):
    return pl.ds(pl.multiple_of(quarter * width, 128), width)


def exchange_kernel(n_exp, n_seq, chosen, grad, ids, group, send_i, recv_i, send_g, recv_g, local):
    g, s = lax.axis_index("exp"), lax.axis_index("seq")
    width = grad.shape[1] // n_seq
    greet([(flip(g, k), s) for k in range(1, n_exp)] + [(g, flip(s, k)) for k in range(1, n_seq)])
    copies = []
    for k in range(1, n_exp):
        copies.append(remote(chosen, ids.at[g], send_i.at[k], recv_i.at[k], (flip(g, k), s)))
        copies[-1].start()
    for k in range(n_seq - 1, 0, -1):
        t = flip(s, k)
        copies.append(
            remote(grad.at[:, columns(t, width)], group.at[s], send_g.at[k], recv_g.at[k], (g, t))
        )
        copies[-1].start()
    own_ids = pltpu.make_async_copy(chosen, ids.at[g], local.at[0])
    own_grad = pltpu.make_async_copy(grad.at[:, columns(s, width)], group.at[s], local.at[1])
    own_ids.start()
    own_grad.start()
    for c in copies:
        c.wait()
    own_ids.wait()
    own_grad.wait()


def exchange(n_exp, n_seq, chosen, grad):
    rows, width = grad.shape[0], grad.shape[1] // n_seq
    dma = pltpu.SemaphoreType.DMA
    return pl.pallas_call(
        functools.partial(exchange_kernel, n_exp, n_seq),
        out_shape=(
            jax.ShapeDtypeStruct((n_exp,) + chosen.shape, chosen.dtype),
            jax.ShapeDtypeStruct((n_seq, rows, width), grad.dtype),
        ),
        in_specs=[VMEM, VMEM],
        out_specs=(VMEM, VMEM),
        scratch_shapes=[dma((n_exp,)), dma((n_exp,)), dma((n_seq,)), dma((n_seq,)), dma((2,))],
        compiler_params=pltpu.CompilerParams(collective_id=0, has_side_effects=True),
    )(chosen, grad)


def dispatch_kernel(n_exp, out, fetched, s0, r0, sa, ra, sb, rb, sc, rc, local):
    g, s = lax.axis_index("exp"), lax.axis_index("seq")
    width = out.shape[2]
    across, beside = (g, flip(s, 2)), (g, flip(s, 1))
    own, theirs = columns(s, width), columns(flip(s, 2), width)
    greet([(flip(g, k), s) for k in range(1, n_exp)] + [across, beside])
    first = pltpu.make_async_copy(out.at[g], fetched.at[g, :, own], local)
    first.start()
    half = n_exp // 2
    order = []
    for k in range(half):
        order.append(half + k)
        if k:
            order.append(k)
    sends = {}
    for k in order:
        e = flip(g, k)
        sends[k] = remote(out.at[e], fetched.at[g, :, own], s0.at[k], r0.at[k], (e, s))
        sends[k].start()
    crossed, done = [], []
    for k in range(n_exp):
        block = fetched.at[flip(g, k)]
        if k:
            sends[k].wait_recv()
        else:
            first.wait()
        c = remote(block.at[:, own], block.at[:, own], sa.at[k], ra.at[k], across)
        c.start()
        crossed.append(c)
        d = remote(block.at[:, own], block.at[:, own], sb.at[k], rb.at[k], beside)
        d.start()
        done.append(d)
    for k in range(n_exp):
        block = fetched.at[flip(g, k)]
        crossed[k].wait_recv()
        d = remote(block.at[:, theirs], block.at[:, theirs], sc.at[k], rc.at[k], beside)
        d.start()
        done.append(d)
    for k in order:
        sends[k].wait_send()
    for c in crossed:
        c.wait_send()
    for d in done:
        d.wait()


def dispatch(n_exp, n_seq, out):
    rows, width = out.shape[1:]
    dma = pltpu.SemaphoreType.DMA
    return pl.pallas_call(
        functools.partial(dispatch_kernel, n_exp),
        out_shape=jax.ShapeDtypeStruct((n_exp, rows, n_seq * width), out.dtype),
        in_specs=[ANY],
        out_specs=ANY,
        scratch_shapes=[dma((n_exp,))] * 8 + [dma],
        compiler_params=pltpu.CompilerParams(collective_id=1, has_side_effects=True),
    )(out)


def combine_kernel(n_exp, part, arrived, near, sum1, far, sum2, s1, r1, s2, r2, s3, r3, local):
    g, s = lax.axis_index("exp"), lax.axis_index("seq")
    width = arrived.shape[2]
    across, beside = (g, flip(s, 2)), (g, flip(s, 1))
    own, theirs = columns(s, width), columns(flip(s, 2), width)
    greet([(flip(g, k), s) for k in range(1, n_exp)] + [across, beside])
    half = n_exp // 2
    order = list(range(half, n_exp)) + list(range(1, half)) + [0]
    pairs = {}
    for k in order:
        e = flip(g, k)
        pairs[k] = [
            remote(
                part.at[e, :, columns(flip(s, bits), width)],
                near.at[e, i],
                s1.at[k, i],
                r1.at[k, i],
                beside,
            )
            for i, bits in enumerate((3, 1))
        ]
        for c in pairs[k]:
            c.start()
    middle, last = {}, {}
    for k in order:
        e = flip(g, k)
        pairs[k][0].wait_recv()
        both = part[e, :, theirs].astype(jnp.float32) + near[e, 0].astype(jnp.float32)
        sum1[e] = both.astype(jnp.bfloat16)
        middle[k] = remote(sum1.at[e], far.at[e], s2.at[k], r2.at[k], across)
        middle[k].start()
    for k in order:
        e = flip(g, k)
        pairs[k][1].wait_recv()
        middle[k].wait_recv()
        total = part[e, :, own].astype(jnp.float32) + near[e, 1].astype(jnp.float32)
        total = total + far[e].astype(jnp.float32)
        sum2[e] = total.astype(jnp.bfloat16)
        if k:
            last[k] = remote(sum2.at[e], arrived.at[g], s3.at[k], r3.at[k], (e, s))
        else:
            last[k] = pltpu.make_async_copy(sum2.at[e], arrived.at[g], local)
        last[k].start()
    for k in order:
        for c in pairs[k]:
            c.wait_send()
        middle[k].wait_send()
        last[k].wait()


def combine(n_exp, n_seq, part):
    rows, width = part.shape[1], part.shape[2] // n_seq
    dma = pltpu.SemaphoreType.DMA
    block = pltpu.VMEM((n_exp, rows, width), part.dtype)
    return pl.pallas_call(
        functools.partial(combine_kernel, n_exp),
        out_shape=jax.ShapeDtypeStruct((n_exp, rows, width), part.dtype),
        in_specs=[VMEM],
        out_specs=VMEM,
        scratch_shapes=[pltpu.VMEM((n_exp, 2, rows, width), part.dtype), block, block, block]
        + [dma((n_exp, 2))] * 2
        + [dma((n_exp,))] * 4
        + [dma],
        compiler_params=pltpu.CompilerParams(
            collective_id=2, has_side_effects=True, vmem_limit_bytes=48 * 2**20
        ),
    )(part)


def running_count(hits):
    rows, length = hits.shape
    ahead = lax.broadcasted_iota(jnp.int32, (128, 128), 0)
    here = lax.broadcasted_iota(jnp.int32, (128, 128), 1)
    upper = (ahead <= here).astype(jnp.float32).astype(jnp.bfloat16)
    hits = hits.astype(jnp.float32)
    before = jnp.zeros((rows, 1), jnp.float32)
    out = []
    for j in range(length // 128):
        block = hits[:, j * 128 : (j + 1) * 128]
        count = jnp.dot(block.astype(jnp.bfloat16), upper, preferred_element_type=jnp.float32)
        out.append(count + before)
        before = before + jnp.sum(block, axis=1, keepdims=True)
    return jnp.concatenate(out, axis=1)


ORDER = [
    "mix 0", "csend 5 0", "taket", "mix 1", "csend 5 1", "csend 4 1", "ssend 2 0", "ssend 1 0",
    "csend 4 0", "mix 2", "spread 5 0", "place", "ssend 2 1", "mix 3", "csend 6 0", "mix 4",
    "csend 7 0", "ssend 1 1", "spread 5 1", "ssend 0 0", "ssend 3 1", "csend 7 1", "mix 5",
    "spread 4 1", "mix 6", "fwd 1 0", "fwd 2 0", "turn 5 0", "turn 5 1", "mix 7", "mix 8", "mix 9",
    "fwd 1 1", "ready", "turn 4 1", "fwd 2 1", "spread 4 0", "compute 5", "ssend 3 0", "turn 4 0",
    "fwd 0 0", "compute 2", "spread 6 0", "ssend 0 1", "fwd 0 1", "hand 5 1", "hand 5 0",
    "csend 6 1", "compute 4", "spread 7 0", "turn 6 0", "compute 1", "fwd 3 1", "hand 4 1",
    "spread 7 1", "give 5 0", "fwd 3 0", "gives 2 0", "compute 0", "gives 1 0", "spread 6 1",
    "compute 3", "give 4 1", "gives 0 1", "turn 7 1", "turn 6 1", "give 5 1", "turn 7 0",
    "hand 4 0", "gives 3 0", "compute 6", "compute 7", "hand 6 1", "gives 1 1", "gives 2 1",
    "gives 3 1", "give 4 0", "hand 7 1", "gives 0 0", "hand 7 0", "hand 6 0", "score", "give 6 1",
    "give 7 1", "give 6 0", "finish_s", "give 7 0", "finish_x 1", "finish_x 0",
]


def plan():
    for step in ORDER:
        name, *numbers = step.split()
        yield name, [int(n) for n in numbers]


def layer_kernel(
    n_exp, group_tok, grad, chosen, scores, pre_in, mixing_in, down_in, same_out, cross_out, score_out,
    ids, group, rank, place1, weight, take, take_t, spot, pre, pre_pad, mixing, down, raw,
    fetched, both, part, out_s, out_x, near_s, near, far, sum2, arrived_s, arrived_x, acc_x,
    score_acc, dma, dma_s, dma_r,
):
    g, s = lax.axis_index("exp"), lax.axis_index("seq")
    half = n_exp // 2
    rows = take.shape[1]
    width = group.shape[2]
    own_tok = group_tok // 4
    hw = width // PIECES
    hidden_part = down.shape[0]
    y, c = s // 2, s % 2
    hg, pg = g // half, g % half
    across, beside = (g, flip(s, 2)), (g, flip(s, 1))
    own, theirs = columns(s, width), columns(flip(s, 2), width)
    expert_at = [flip(g, k) for k in range(n_exp)]
    seq_at = [flip(s, k) for k in range(4)]
    count = {"n": 0, "local": 0}
    halves = [pl.ds(h * hw, hw) for h in range(PIECES)]

    def cols(quarter, h):
        return pl.ds(pl.multiple_of(quarter * width + h * hw, 128), hw)

    def remote_to(src, dst, to):
        n = count["n"]
        count["n"] = n + 1
        return remote(src, dst, dma_s.at[n], dma_r.at[n], to)

    def local_copy(src, dst):
        n = count["local"]
        count["local"] = n + 1
        return pltpu.make_async_copy(src, dst, dma.at[n])

    get_down = local_copy(down_in, down)
    step_rows = raw.shape[1]
    raw_parts = [(src, dst, i) for src, dst in ((pre_in, pre), (mixing_in, mixing))
                 for i in range(dst.shape[0] // step_rows)]
    raw_copies = [
        local_copy(src.at[pl.ds(i * step_rows, step_rows)], raw.at[n % 2])
        for n, (src, _, i) in enumerate(raw_parts)
    ]
    greet([(e, s) for e in expert_at[1:]] + [(g, t) for t in seq_at[1:]])
    id_sends, first, second = [], {}, []
    side = (y, 1 - y)
    for k in range(1, n_exp):
        id_sends.append(remote_to(chosen, ids.at[g], (expert_at[k], s)))
        id_sends[-1].start()
    mine = pl.ds(pl.multiple_of(s * own_tok, own_tok), own_tok)
    for h in range(PIECES):
        for k in (2, 3, 1):
            t = seq_at[k]
            first[k, h] = remote_to(
                grad.at[:, cols(t, h)], group.at[t // 2, mine, halves[h]], (g, t)
            )
            first[k, h].start()
    for k in (2, 3, 1):
        t = seq_at[k]
        second.append(
            remote_to(grad.at[:, columns(flip(t, 2), width)], group.at[1 - t // 2, mine], (g, t))
        )
        second[-1].start()
    own_copies = [
        local_copy(chosen, ids.at[g]),
        local_copy(grad.at[:, own], group.at[y, mine]),
        local_copy(grad.at[:, theirs], group.at[1 - y, mine]),
    ]
    for d in own_copies:
        d.start()
    get_down.start()
    raw_copies[0].start()

    capacity = chosen.shape[1]
    row = lax.broadcasted_iota(jnp.int32, (n_exp, capacity), 0)
    slot = lax.broadcasted_iota(jnp.int32, (rows, capacity), 0).astype(jnp.float32)

    for d in id_sends:
        d.wait_recv()
    own_copies[0].wait()
    local = jnp.zeros((n_exp, capacity), jnp.int32)
    for e in range(n_exp):
        local = jnp.where(row == e, ids[e], local)
    local = local - g * group_tok
    inside = (local >= 0) & (local < group_tok)
    rank[0] = jnp.where(inside, running_count(inside) - 1.0, -1.0)
    rank[1] = (local + 1).astype(jnp.float32)

    @pl.loop(0, n_exp)
    def _(e):
        picked = rank[0, pl.ds(e, 1), :] == slot
        at = jnp.sum(jnp.where(picked, rank[1, pl.ds(e, 1), :], 0.0), axis=1, keepdims=True) - 1.0
        spot[e] = at
        token = lax.broadcasted_iota(jnp.int32, (rows, group_tok), 1).astype(jnp.float32)
        take[e] = (at == token).astype(jnp.float32).astype(jnp.bfloat16)

    def select(e, q):
        return jnp.dot(take[e], group[q], preferred_element_type=jnp.float32).astype(jnp.bfloat16)

    sends, sends_s, moved_s = {}, {}, {}
    crossed, moved, turned, pairs, middle, last, ends = {}, {}, {}, {}, {}, {}, []
    seen = set()
    score_acc[...] = jnp.zeros_like(score_acc)

    def once(*key):
        new = key not in seen
        seen.add(key)
        return new

    def csend(k, h):
        if once("own"):
            own_copies[1].wait()
        if once("first", h):
            for j in (2, 3, 1):
                first[j, h].wait_recv()
        e = expert_at[k]
        out_x[k - half, :, halves[h]] = jnp.dot(
            take[e], group[y, :, halves[h]], preferred_element_type=jnp.float32
        ).astype(jnp.bfloat16)
        sends[k, h] = remote_to(
            out_x.at[k - half, :, halves[h]], fetched.at[g, :, cols(s, h)], (e, s)
        )
        sends[k, h].start()

    def ssend(k, i):
        if once("own"):
            own_copies[1].wait()
        if i == 0:
            for h in range(PIECES):
                if once("first", h):
                    for j in (2, 3, 1):
                        first[j, h].wait_recv()
        elif once("second"):
            for d in second:
                d.wait_recv()
            own_copies[2].wait()
        e = expert_at[k]
        if k:
            here = pl.ds(i * width, width)
            out_s[k, :, here] = select(e, side[i])
            sends_s[k, i] = remote_to(
                out_s.at[k, :, here], fetched.at[g, :, columns(flip(s, 2 * i), width)], (e, s)
            )
            sends_s[k, i].start()
        else:
            fetched[g, :, columns(flip(s, 2 * i), width)] = select(e, side[i])

    def mix(n):
        if n + 1 < len(raw_copies):
            raw_copies[n + 1].start()
        raw_copies[n].wait()
        _, dst, i = raw_parts[n]
        dst[i * step_rows : (i + 1) * step_rows, :] = raw[n % 2].reshape(
            step_rows, 2 * hidden_part
        )

    def place():
        ids_here = chosen[...]
        low = row * group_tok
        hits = (ids_here >= low) & (ids_here < low + group_tok)
        rank[2] = jnp.where(hits, running_count(hits) - 1.0, -1.0)

        @pl.loop(0, n_exp)
        def _(e):
            picked = rank[2, pl.ds(e, 1), :] == slot
            place1[e] = picked.astype(jnp.float32).astype(jnp.bfloat16)
            weight[e] = jnp.sum(jnp.where(picked, scores[...], 0.0), axis=1, keepdims=True)
            pre_pad[e] = jnp.dot(
                place1[e], pre[...], preferred_element_type=jnp.float32
            ).astype(jnp.bfloat16)

    def taket():
        @pl.loop(0, 2)
        def _(h):
            at = spot[pl.ds(h * half, half)].reshape(half * rows, 1)
            a = lax.broadcasted_iota(jnp.int32, (half * rows, half * rows), 0)
            b = lax.broadcasted_iota(jnp.int32, (half * rows, half * rows), 1)
            flat = jnp.sum(jnp.where(a == b, at, 0.0), axis=0, keepdims=True)
            token = lax.broadcasted_iota(jnp.int32, (group_tok, half * rows), 0)
            token = token.astype(jnp.float32)
            take_t[h] = (token == flat).astype(jnp.float32).astype(jnp.bfloat16)

    def ready():
        get_down.wait()

    def fwd(k, i):
        if k:
            sends_s[k, i].wait_recv()
        block = fetched.at[expert_at[k], :, columns(flip(s, 2 * i), width)]
        moved_s[k, i] = remote_to(block, block, beside)
        moved_s[k, i].start()

    def spread(k, h):
        block = fetched.at[expert_at[k], :, cols(s, h)]
        sends[k, h].wait_recv()
        crossed[k, h] = remote_to(block, block, across)
        crossed[k, h].start()
        moved[k, h] = remote_to(block, block, beside)
        moved[k, h].start()

    def turn(k, h):
        block = fetched.at[expert_at[k], :, cols(flip(s, 2), h)]
        crossed[k, h].wait_recv()
        turned[k, h] = remote_to(block, block, beside)
        turned[k, h].start()

    def compute(k):
        e = expert_at[k]
        if k < half:
            for i in range(2):
                moved_s[k, i].wait_recv()
        else:
            for h in range(PIECES):
                moved[k, h].wait_recv()
                turned[k, h].wait_recv()
        back = lax.dot_general(
            fetched[e], down[...], (((1,), (1,)), ((), ())), preferred_element_type=jnp.float32
        )
        gate_pre = pre_pad[e, :, :hidden_part].astype(jnp.float32)
        up_pre = pre_pad[e, :, hidden_part:].astype(jnp.float32)
        sigmoid_gate = jax.nn.sigmoid(gate_pre)
        activated = gate_pre * sigmoid_gate
        hidden = (activated * up_pre).astype(jnp.bfloat16)
        value = jnp.sum(hidden.astype(jnp.float32) * back, axis=1, keepdims=True)
        here = place1[e].astype(jnp.float32) > 0.5
        score_acc[...] += jnp.sum(jnp.where(here, value, 0.0), axis=0, keepdims=True)
        scaled = weight[e] * back
        d_gate = scaled * up_pre * sigmoid_gate * (1.0 + gate_pre * (1.0 - sigmoid_gate))
        both[:, :hidden_part] = d_gate.astype(jnp.bfloat16)
        both[:, hidden_part:] = (scaled * activated).astype(jnp.bfloat16)

        @pl.loop(0, mixing.shape[0] // 512)
        def _(i):
            tile = columns(i, 512)
            part[e, :, tile] = lax.dot_general(
                both[...],
                mixing[tile, :],
                (((1,), (1,)), ((), ())),
                preferred_element_type=jnp.float32,
            ).astype(jnp.bfloat16)

        p = e % half
        if k < half:
            pairs[k] = [
                remote_to(
                    part.at[e, :, columns(flip(s, 2 * i + 1), width)],
                    near_s.at[p, :, pl.ds(i * width, width)],
                    beside,
                )
                for i in range(2)
            ]
        else:
            pairs[k] = [
                remote_to(part.at[e, :, columns(flip(s, bits), width)], near.at[p, i], beside)
                for i, bits in enumerate((3, 1))
            ]
        for d in pairs[k]:
            d.start()

    def gives(k, i):
        e = expert_at[k]
        p = e % half
        here = pl.ds(i * width, width)
        pairs[k][i].wait_recv()
        value = part[e, :, columns(flip(s, 2 * i), width)].astype(jnp.float32)
        value = (value + near_s[p, :, here].astype(jnp.float32)).astype(jnp.bfloat16)
        if k:
            sends_s[k, i].wait_send()
            out_s[k, :, here] = value
            last[k, i] = remote_to(out_s.at[k, :, here], arrived_s.at[pg, :, here], (e, s))
            last[k, i].start()
        else:
            arrived_s[pg, :, here] = value

    def hand(k, h):
        e = expert_at[k]
        p = e % half
        if once("pair", k, 0):
            pairs[k][0].wait_recv()
        sends[k, h].wait_send()
        value = part[e, :, cols(flip(s, 2), h)].astype(jnp.float32)
        value = value + near[p, 0, :, halves[h]].astype(jnp.float32)
        out_x[k - half, :, halves[h]] = value.astype(jnp.bfloat16)
        middle[k, h] = remote_to(
            out_x.at[k - half, :, halves[h]], far.at[p, :, halves[h]], across
        )
        middle[k, h].start()

    def give(k, h):
        e = expert_at[k]
        p = e % half
        if once("pair", k, 1):
            pairs[k][1].wait_recv()
        middle[k, h].wait_recv()
        value = part[e, :, cols(s, h)].astype(jnp.float32)
        value = value + near[p, 1, :, halves[h]].astype(jnp.float32)
        value = value + far[p, :, halves[h]].astype(jnp.float32)
        sum2[p, :, halves[h]] = value.astype(jnp.bfloat16)
        last[k, h] = remote_to(
            sum2.at[p, :, halves[h]], arrived_x.at[pg, :, halves[h]], (e, s)
        )
        last[k, h].start()

    def score():
        for j in range(1, 4):
            ends.append(remote_to(score_acc, score_out.at[s], (g, seq_at[j])))
            ends[-1].start()
        ends.append(local_copy(score_acc, score_out.at[s]))
        ends[-1].start()

    def token_block(j):
        return pl.ds(pl.multiple_of(seq_at[j] * own_tok, own_tok), own_tok)

    def finish_s():
        for j in range(1, half):
            last[j, 1].wait_recv()
        terms = arrived_s[:, :, width:].reshape(half * rows, width)
        group[0] = jnp.dot(
            take_t[hg], terms, preferred_element_type=jnp.float32
        ).astype(jnp.bfloat16)
        for j in (2, 3, 1, 0):
            src = group.at[0, token_block(j)]
            dst = same_out.at[:, theirs]
            ends.append(remote_to(src, dst, (g, seq_at[j])) if j else local_copy(src, dst))
            ends[-1].start()

    def finish_x(h):
        if once("near"):
            for j in range(1, half):
                last[j, 0].wait_recv()
        for j in range(half, n_exp):
            last[j, h].wait_recv()
        terms = arrived_x[:, :, halves[h]].reshape(half * rows, hw)
        value = jnp.dot(take_t[1 - hg], terms, preferred_element_type=jnp.float32)
        terms = arrived_s[:, :, halves[h]].reshape(half * rows, hw)
        value = value + jnp.dot(take_t[hg], terms, preferred_element_type=jnp.float32)
        acc_x[:, halves[h]] = value.astype(jnp.bfloat16)
        for j in (2, 3, 1, 0):
            src = acc_x.at[token_block(j), halves[h]]
            dst = cross_out.at[:, cols(s, h)]
            ends.append(remote_to(src, dst, (g, seq_at[j])) if j else local_copy(src, dst))
            ends[-1].start()

    steps = {
        "csend": csend, "ssend": ssend, "mix": mix, "place": place, "taket": taket, "ready": ready,
        "fwd": fwd, "spread": spread, "turn": turn, "compute": compute, "gives": gives,
        "hand": hand, "give": give, "score": score, "finish_s": finish_s, "finish_x": finish_x,
    }
    for step, numbers in plan():
        steps[step](*numbers)
    for d in id_sends + second:
        d.wait_send()
    for group_of in (first, crossed, moved, turned, moved_s, middle, last):
        for d in group_of.values():
            d.wait_send()
    for k in range(n_exp):
        for d in pairs[k]:
            d.wait_send()
    for d in ends:
        d.wait()


def layer(n_exp, out_grad, chosen, scores, pre, mixing, down):
    own_tok, model_width = out_grad.shape
    capacity = chosen.shape[1]
    width = model_width // 4
    group_tok = own_tok * 4
    rows = 9 * capacity // (8 * n_exp)
    half = n_exp // 2
    hidden2 = 2 * mixing.shape[2]
    step_rows = 512
    kind = out_grad.dtype
    dma = pltpu.SemaphoreType.DMA
    f32 = jnp.float32

    def v(*shape, dtype=kind):
        return pltpu.VMEM(shape, dtype)

    total = 30 * PIECES + 60
    return pl.pallas_call(
        functools.partial(layer_kernel, n_exp, group_tok),
        out_shape=(
            jax.ShapeDtypeStruct((own_tok, model_width), kind),
            jax.ShapeDtypeStruct((own_tok, model_width), kind),
            jax.ShapeDtypeStruct((4, 1, capacity), f32),
        ),
        in_specs=[ANY, VMEM, VMEM, ANY, ANY, ANY],
        out_specs=(ANY, ANY, VMEM),
        scratch_shapes=[
            v(n_exp, 1, capacity, dtype=jnp.int32),
            v(2, group_tok, width),
            v(3, n_exp, capacity, dtype=f32),
            v(n_exp, rows, capacity),
            v(n_exp, rows, 1, dtype=f32),
            v(n_exp, rows, group_tok),
            v(2, group_tok, half * rows),
            v(n_exp, rows, 1, dtype=f32),
            v(capacity, hidden2),
            v(n_exp, rows, hidden2),
            v(model_width, hidden2),
            v(hidden2 // 2, model_width),
            v(2, step_rows, 2, hidden2 // 2),
            v(n_exp, rows, model_width),
            v(rows, hidden2),
            v(n_exp, rows, model_width),
            v(half, rows, 2 * width),
            v(half, rows, width),
            v(half, rows, 2 * width),
            v(half, 2, rows, width),
            v(half, rows, width),
            v(half, rows, width),
            v(half, rows, 2 * width),
            v(half, rows, width),
            v(group_tok, width),
            v(1, capacity, dtype=f32),
            dma((24,)),
            dma((total,)),
            dma((total,)),
        ],
        compiler_params=pltpu.CompilerParams(
            collective_id=4, has_side_effects=True, vmem_limit_bytes=60 * 2**20
        ),
    )(out_grad, chosen, scores, pre, mixing, down)


def regroup_kernel(
    n_seq, totals, score, out, score_sum, scores, send, recv, send_s, recv_s, local
):
    g, s = lax.axis_index("exp"), lax.axis_index("seq")
    width = totals.shape[2]
    own = columns(s, width)
    greet([(g, flip(s, k)) for k in range(1, n_seq)])
    copies = []
    for k in range(n_seq - 1, 0, -1):
        t = flip(s, k)
        copies.append(remote(totals.at[t], out.at[:, own], send.at[k], recv.at[k], (g, t)))
        copies[-1].start()
        copies.append(remote(score, scores.at[s], send_s.at[k], recv_s.at[k], (g, t)))
        copies[-1].start()
    mine = pltpu.make_async_copy(totals.at[s], out.at[:, own], local)
    mine.start()
    scores[s] = score[...]
    for c in copies:
        c.wait()
    value = scores[0]
    for k in range(1, n_seq):
        value = value + scores[k]
    score_sum[...] = value
    mine.wait()


def regroup(n_seq, totals, score):
    rows, width = totals.shape[1:]
    dma = pltpu.SemaphoreType.DMA
    return pl.pallas_call(
        functools.partial(regroup_kernel, n_seq),
        out_shape=(
            jax.ShapeDtypeStruct((rows, n_seq * width), totals.dtype),
            jax.ShapeDtypeStruct(score.shape, score.dtype),
        ),
        in_specs=[VMEM, VMEM],
        out_specs=(VMEM, VMEM),
        scratch_shapes=[pltpu.VMEM((n_seq,) + score.shape, score.dtype)]
        + [dma((n_seq,))] * 4
        + [dma],
        compiler_params=pltpu.CompilerParams(collective_id=3, has_side_effects=True),
    )(totals, score)


def counts(hits):
    length = hits.shape[1]
    at = jnp.arange(length, dtype=jnp.int32)
    upper = (at[:, None] <= at[None, :]).astype(jnp.bfloat16)
    total = jnp.dot(hits.astype(jnp.bfloat16), upper, preferred_element_type=jnp.float32)
    return total.astype(jnp.int32)


def local(out_grad, chosen, scores, saved_pre, gate_up, down):
    n_exp = lax.axis_size("exp")
    n_seq = lax.axis_size("seq")
    capacity = chosen.shape[1]
    slot_most = 9 * capacity // (8 * n_exp)
    tok_count, model_width = out_grad.shape
    width = model_width // n_seq
    group_tok = tok_count * n_seq
    pad_rows = n_exp * slot_most
    hidden_part = gate_up.shape[3]
    group_index = lax.axis_index("exp")

    if slot_most % 16 == 0 and n_exp == 8 and n_seq == 4:
        same, cross, score_parts = layer(
            n_exp,
            out_grad,
            chosen,
            scores,
            saved_pre[0],
            gate_up[0],
            down[0],
        )
        value = same.astype(jnp.float32) + cross.astype(jnp.float32)
        return value.astype(jnp.bfloat16), jnp.sum(score_parts, axis=0)

    own_ids = chosen[0]
    owner_group = own_ids // group_tok
    owner_hits = (owner_group[None, :] == jnp.arange(n_exp, dtype=jnp.int32)[:, None]).astype(
        jnp.int32
    )
    slot_order = jnp.sum(counts(owner_hits) * owner_hits, axis=0) - 1
    position = owner_group * slot_most + slot_order
    place = position[None, :] == jnp.arange(pad_rows, dtype=jnp.int32)[:, None]
    weight_padded = jnp.sum(jnp.where(place, scores[0][None, :], 0.0), axis=1)
    place_one = place.astype(jnp.bfloat16)

    def padded(x):
        return jnp.dot(place_one, x, preferred_element_type=jnp.float32)

    gate_pre = padded(saved_pre[0, :, 0])
    up_pre = padded(saved_pre[0, :, 1])
    mixing = gate_up[0].reshape(model_width, 2 * hidden_part)

    ids, group = exchange(n_exp, n_seq, chosen.reshape(capacity // 128, 128), out_grad)
    local_ids = ids.reshape(n_exp, capacity) - group_index * group_tok
    inside = (local_ids >= 0) & (local_ids < group_tok)
    slot_rank = counts(inside) - 1
    slot_ids = jnp.arange(slot_most, dtype=jnp.int32)
    picked = inside[:, None, :] & (slot_rank[:, None, :] == slot_ids[None, :, None])
    source = jnp.sum(jnp.where(picked, local_ids[:, None, :] + 1, 0), axis=2).reshape(pad_rows) - 1
    tokens = jnp.arange(group_tok, dtype=jnp.int32)
    take = (source[:, None] == tokens[None, :]).astype(jnp.bfloat16)
    outgoing = jnp.dot(
        take, group.reshape(group_tok, width), preferred_element_type=jnp.float32
    ).astype(jnp.bfloat16)
    outgoing = outgoing.reshape(n_exp, slot_most, width)
    fetched = dispatch(n_exp, n_seq, outgoing)
    fetched = fetched.reshape(pad_rows, model_width)

    back_grad = lax.dot_general(
        fetched, down[0], (((1,), (1,)), ((), ())), preferred_element_type=jnp.float32
    )
    sigmoid_gate = jax.nn.sigmoid(gate_pre)
    activated = gate_pre * sigmoid_gate
    hidden = (activated * up_pre).astype(jnp.bfloat16)
    hidden = lax.optimization_barrier(hidden)
    score_part = jnp.sum(hidden.astype(jnp.float32) * back_grad, axis=1)
    scaled = weight_padded[:, None] * back_grad
    d_gate = scaled * up_pre * sigmoid_gate * (1.0 + gate_pre * (1.0 - sigmoid_gate))
    d_up = scaled * activated
    d_both = jnp.concatenate([d_gate, d_up], axis=1).astype(jnp.bfloat16)
    partial_value = lax.dot_general(
        d_both, mixing, (((1,), (1,)), ((), ())), preferred_element_type=jnp.float32
    ).astype(jnp.bfloat16)
    arrived = combine(n_exp, n_seq, partial_value.reshape(n_exp, slot_most, model_width))
    score_slots = jnp.sum(jnp.where(place, score_part[:, None], 0.0), axis=0)
    totals = lax.dot_general(
        take,
        arrived.reshape(pad_rows, width),
        (((0,), (0,)), ((), ())),
        preferred_element_type=jnp.float32,
    ).astype(jnp.bfloat16)
    summed, score_grad = regroup(
        n_seq,
        totals.reshape(n_seq, tok_count, width),
        score_slots.reshape(capacity // 128, 128),
    )
    return (summed, score_grad.reshape(1, capacity))


def solution(mesh):
    return jax.shard_map(
        local,
        mesh=mesh,
        in_specs=(
            P(("exp", "seq"), None),
            P("exp", None),
            P("exp", None),
            P("exp", None, None, "seq"),
            P("exp", None, None, "seq"),
            P("exp", "seq", None),
        ),
        out_specs=(P(("exp", "seq"), None), P("exp", None)),
        check_vma=False,
    )
```

```python
import functools

import jax
import jax.numpy as jnp
from jax import lax
from jax.experimental import pallas as pl
from jax.experimental.pallas import tpu as pltpu
from jax.sharding import PartitionSpec as P

MESH = pl.DeviceIdType.MESH
PIECES = 2
ANY = pl.BlockSpec(memory_space=pl.ANY)
VMEM = pl.BlockSpec(memory_space=pltpu.VMEM)


def flip(index, bits):
    out, step = index, 1
    while bits >= step:
        if bits & step:
            out = out + step * (1 - 2 * ((index // step) % 2))
        step *= 2
    return out


def greet(peers):
    barrier = pltpu.get_barrier_semaphore()
    for p in peers:
        pl.semaphore_signal(barrier, inc=1, device_id=p, device_id_type=MESH)
    pl.semaphore_wait(barrier, len(peers))


def remote(src, dst, send, recv, to):
    return pltpu.make_async_remote_copy(
        src_ref=src, dst_ref=dst, send_sem=send, recv_sem=recv, device_id=to, device_id_type=MESH
    )


def columns(quarter, width):
    return pl.ds(pl.multiple_of(quarter * width, 128), width)


def exchange_kernel(n_exp, n_seq, chosen, grad, ids, group, send_i, recv_i, send_g, recv_g, local):
    g, s = lax.axis_index("exp"), lax.axis_index("seq")
    width = grad.shape[1] // n_seq
    greet([(flip(g, k), s) for k in range(1, n_exp)] + [(g, flip(s, k)) for k in range(1, n_seq)])
    copies = []
    for k in range(1, n_exp):
        copies.append(remote(chosen, ids.at[g], send_i.at[k], recv_i.at[k], (flip(g, k), s)))
        copies[-1].start()
    for k in range(n_seq - 1, 0, -1):
        t = flip(s, k)
        copies.append(
            remote(grad.at[:, columns(t, width)], group.at[s], send_g.at[k], recv_g.at[k], (g, t))
        )
        copies[-1].start()
    own_ids = pltpu.make_async_copy(chosen, ids.at[g], local.at[0])
    own_grad = pltpu.make_async_copy(grad.at[:, columns(s, width)], group.at[s], local.at[1])
    own_ids.start()
    own_grad.start()
    for c in copies:
        c.wait()
    own_ids.wait()
    own_grad.wait()


def exchange(n_exp, n_seq, chosen, grad):
    rows, width = grad.shape[0], grad.shape[1] // n_seq
    dma = pltpu.SemaphoreType.DMA
    return pl.pallas_call(
        functools.partial(exchange_kernel, n_exp, n_seq),
        out_shape=(
            jax.ShapeDtypeStruct((n_exp,) + chosen.shape, chosen.dtype),
            jax.ShapeDtypeStruct((n_seq, rows, width), grad.dtype),
        ),
        in_specs=[VMEM, VMEM],
        out_specs=(VMEM, VMEM),
        scratch_shapes=[dma((n_exp,)), dma((n_exp,)), dma((n_seq,)), dma((n_seq,)), dma((2,))],
        compiler_params=pltpu.CompilerParams(collective_id=0, has_side_effects=True),
    )(chosen, grad)


def dispatch_kernel(n_exp, out, fetched, s0, r0, sa, ra, sb, rb, sc, rc, local):
    g, s = lax.axis_index("exp"), lax.axis_index("seq")
    width = out.shape[2]
    across, beside = (g, flip(s, 2)), (g, flip(s, 1))
    own, theirs = columns(s, width), columns(flip(s, 2), width)
    greet([(flip(g, k), s) for k in range(1, n_exp)] + [across, beside])
    first = pltpu.make_async_copy(out.at[g], fetched.at[g, :, own], local)
    first.start()
    half = n_exp // 2
    order = []
    for k in range(half):
        order.append(half + k)
        if k:
            order.append(k)
    sends = {}
    for k in order:
        e = flip(g, k)
        sends[k] = remote(out.at[e], fetched.at[g, :, own], s0.at[k], r0.at[k], (e, s))
        sends[k].start()
    crossed, done = [], []
    for k in range(n_exp):
        block = fetched.at[flip(g, k)]
        if k:
            sends[k].wait_recv()
        else:
            first.wait()
        c = remote(block.at[:, own], block.at[:, own], sa.at[k], ra.at[k], across)
        c.start()
        crossed.append(c)
        d = remote(block.at[:, own], block.at[:, own], sb.at[k], rb.at[k], beside)
        d.start()
        done.append(d)
    for k in range(n_exp):
        block = fetched.at[flip(g, k)]
        crossed[k].wait_recv()
        d = remote(block.at[:, theirs], block.at[:, theirs], sc.at[k], rc.at[k], beside)
        d.start()
        done.append(d)
    for k in order:
        sends[k].wait_send()
    for c in crossed:
        c.wait_send()
    for d in done:
        d.wait()


def dispatch(n_exp, n_seq, out):
    rows, width = out.shape[1:]
    dma = pltpu.SemaphoreType.DMA
    return pl.pallas_call(
        functools.partial(dispatch_kernel, n_exp),
        out_shape=jax.ShapeDtypeStruct((n_exp, rows, n_seq * width), out.dtype),
        in_specs=[ANY],
        out_specs=ANY,
        scratch_shapes=[dma((n_exp,))] * 8 + [dma],
        compiler_params=pltpu.CompilerParams(collective_id=1, has_side_effects=True),
    )(out)


def combine_kernel(n_exp, part, arrived, near, sum1, far, sum2, s1, r1, s2, r2, s3, r3, local):
    g, s = lax.axis_index("exp"), lax.axis_index("seq")
    width = arrived.shape[2]
    across, beside = (g, flip(s, 2)), (g, flip(s, 1))
    own, theirs = columns(s, width), columns(flip(s, 2), width)
    greet([(flip(g, k), s) for k in range(1, n_exp)] + [across, beside])
    half = n_exp // 2
    order = list(range(half, n_exp)) + list(range(1, half)) + [0]
    pairs = {}
    for k in order:
        e = flip(g, k)
        pairs[k] = [
            remote(
                part.at[e, :, columns(flip(s, bits), width)],
                near.at[e, i],
                s1.at[k, i],
                r1.at[k, i],
                beside,
            )
            for i, bits in enumerate((3, 1))
        ]
        for c in pairs[k]:
            c.start()
    middle, last = {}, {}
    for k in order:
        e = flip(g, k)
        pairs[k][0].wait_recv()
        both = part[e, :, theirs].astype(jnp.float32) + near[e, 0].astype(jnp.float32)
        sum1[e] = both.astype(jnp.bfloat16)
        middle[k] = remote(sum1.at[e], far.at[e], s2.at[k], r2.at[k], across)
        middle[k].start()
    for k in order:
        e = flip(g, k)
        pairs[k][1].wait_recv()
        middle[k].wait_recv()
        total = part[e, :, own].astype(jnp.float32) + near[e, 1].astype(jnp.float32)
        total = total + far[e].astype(jnp.float32)
        sum2[e] = total.astype(jnp.bfloat16)
        if k:
            last[k] = remote(sum2.at[e], arrived.at[g], s3.at[k], r3.at[k], (e, s))
        else:
            last[k] = pltpu.make_async_copy(sum2.at[e], arrived.at[g], local)
        last[k].start()
    for k in order:
        for c in pairs[k]:
            c.wait_send()
        middle[k].wait_send()
        last[k].wait()


def combine(n_exp, n_seq, part):
    rows, width = part.shape[1], part.shape[2] // n_seq
    dma = pltpu.SemaphoreType.DMA
    block = pltpu.VMEM((n_exp, rows, width), part.dtype)
    return pl.pallas_call(
        functools.partial(combine_kernel, n_exp),
        out_shape=jax.ShapeDtypeStruct((n_exp, rows, width), part.dtype),
        in_specs=[VMEM],
        out_specs=VMEM,
        scratch_shapes=[pltpu.VMEM((n_exp, 2, rows, width), part.dtype), block, block, block]
        + [dma((n_exp, 2))] * 2
        + [dma((n_exp,))] * 4
        + [dma],
        compiler_params=pltpu.CompilerParams(
            collective_id=2, has_side_effects=True, vmem_limit_bytes=48 * 2**20
        ),
    )(part)


def running_count(hits):
    rows, length = hits.shape
    ahead = lax.broadcasted_iota(jnp.int32, (128, 128), 0)
    here = lax.broadcasted_iota(jnp.int32, (128, 128), 1)
    upper = (ahead <= here).astype(jnp.float32).astype(jnp.bfloat16)
    hits = hits.astype(jnp.float32)
    before = jnp.zeros((rows, 1), jnp.float32)
    out = []
    for j in range(length // 128):
        block = hits[:, j * 128 : (j + 1) * 128]
        count = jnp.dot(block.astype(jnp.bfloat16), upper, preferred_element_type=jnp.float32)
        out.append(count + before)
        before = before + jnp.sum(block, axis=1, keepdims=True)
    return jnp.concatenate(out, axis=1)


ORDER = [
    "mix 0", "csend 5 0", "taket", "mix 1", "csend 5 1", "csend 4 1", "ssend 2 0", "ssend 1 0",
    "csend 4 0", "mix 2", "spread 5 0", "place", "ssend 2 1", "mix 3", "csend 6 0", "mix 4",
    "csend 7 0", "ssend 1 1", "spread 5 1", "ssend 0 0", "ssend 3 1", "csend 7 1", "mix 5",
    "spread 4 1", "mix 6", "fwd 1 0", "fwd 2 0", "turn 5 0", "turn 5 1", "mix 7", "mix 8", "mix 9",
    "fwd 1 1", "ready", "turn 4 1", "fwd 2 1", "spread 4 0", "compute 5", "ssend 3 0", "turn 4 0",
    "fwd 0 0", "compute 2", "spread 6 0", "ssend 0 1", "fwd 0 1", "hand 5 1", "hand 5 0",
    "csend 6 1", "compute 4", "spread 7 0", "turn 6 0", "compute 1", "fwd 3 1", "hand 4 1",
    "spread 7 1", "give 5 0", "fwd 3 0", "gives 2 0", "give 5 1", "compute 0", "gives 1 0",
    "spread 6 1", "give 4 1", "compute 3", "gives 0 1", "turn 7 1", "turn 6 1", "turn 7 0",
    "hand 4 0", "gives 3 0", "compute 6", "compute 7", "hand 6 1", "gives 1 1", "gives 2 1",
    "gives 3 1", "give 4 0", "hand 7 1", "gives 0 0", "hand 7 0", "hand 6 0", "score", "give 6 1",
    "give 7 1", "give 6 0", "finish_s", "give 7 0", "finish_x 1", "finish_x 0",
]


def plan():
    for step in ORDER:
        name, *numbers = step.split()
        yield name, [int(n) for n in numbers]


def layer_kernel(
    n_exp, group_tok, grad, chosen, scores, pre_in, mixing_in, down_in, same_out, cross_out, score_out,
    ids, group, rank, place1, weight, take, take_t, spot, pre, pre_pad, mixing, down, raw,
    fetched, both, part, out_s, out_x, near_s, near, far, sum2, arrived_s, arrived_x, acc_x,
    score_acc, dma, dma_s, dma_r,
):
    g, s = lax.axis_index("exp"), lax.axis_index("seq")
    half = n_exp // 2
    rows = take.shape[1]
    width = group.shape[2]
    own_tok = group_tok // 4
    hw = width // PIECES
    hidden_part = down.shape[0]
    y, c = s // 2, s % 2
    hg, pg = g // half, g % half
    across, beside = (g, flip(s, 2)), (g, flip(s, 1))
    own, theirs = columns(s, width), columns(flip(s, 2), width)
    expert_at = [flip(g, k) for k in range(n_exp)]
    seq_at = [flip(s, k) for k in range(4)]
    count = {"n": 0, "local": 0}
    halves = [pl.ds(h * hw, hw) for h in range(PIECES)]

    def cols(quarter, h):
        return pl.ds(pl.multiple_of(quarter * width + h * hw, 128), hw)

    def remote_to(src, dst, to):
        n = count["n"]
        count["n"] = n + 1
        return remote(src, dst, dma_s.at[n], dma_r.at[n], to)

    def local_copy(src, dst):
        n = count["local"]
        count["local"] = n + 1
        return pltpu.make_async_copy(src, dst, dma.at[n])

    get_down = local_copy(down_in, down)
    step_rows = raw.shape[1]
    raw_parts = [(src, dst, i) for src, dst in ((pre_in, pre), (mixing_in, mixing))
                 for i in range(dst.shape[0] // step_rows)]
    raw_copies = [
        local_copy(src.at[pl.ds(i * step_rows, step_rows)], raw.at[n % 2])
        for n, (src, _, i) in enumerate(raw_parts)
    ]
    greet([(e, s) for e in expert_at[1:]] + [(g, t) for t in seq_at[1:]])
    id_sends, first, second = [], {}, []
    side = (y, 1 - y)
    for k in range(1, n_exp):
        id_sends.append(remote_to(chosen, ids.at[g], (expert_at[k], s)))
        id_sends[-1].start()
    mine = pl.ds(pl.multiple_of(s * own_tok, own_tok), own_tok)
    for h in range(PIECES):
        for k in (2, 3, 1):
            t = seq_at[k]
            first[k, h] = remote_to(
                grad.at[:, cols(t, h)], group.at[t // 2, mine, halves[h]], (g, t)
            )
            first[k, h].start()
    for k in (2, 3, 1):
        t = seq_at[k]
        second.append(
            remote_to(grad.at[:, columns(flip(t, 2), width)], group.at[1 - t // 2, mine], (g, t))
        )
        second[-1].start()
    own_copies = [
        local_copy(chosen, ids.at[g]),
        local_copy(grad.at[:, own], group.at[y, mine]),
        local_copy(grad.at[:, theirs], group.at[1 - y, mine]),
    ]
    for d in own_copies:
        d.start()
    get_down.start()
    raw_copies[0].start()

    capacity = chosen.shape[1]
    row = lax.broadcasted_iota(jnp.int32, (n_exp, capacity), 0)
    slot = lax.broadcasted_iota(jnp.int32, (rows, capacity), 0).astype(jnp.float32)

    for d in id_sends:
        d.wait_recv()
    own_copies[0].wait()
    local = jnp.zeros((n_exp, capacity), jnp.int32)
    for e in range(n_exp):
        local = jnp.where(row == e, ids[e], local)
    local = local - g * group_tok
    inside = (local >= 0) & (local < group_tok)
    rank[0] = jnp.where(inside, running_count(inside) - 1.0, -1.0)
    rank[1] = (local + 1).astype(jnp.float32)

    @pl.loop(0, n_exp)
    def _(e):
        picked = rank[0, pl.ds(e, 1), :] == slot
        at = jnp.sum(jnp.where(picked, rank[1, pl.ds(e, 1), :], 0.0), axis=1, keepdims=True) - 1.0
        spot[e] = at
        token = lax.broadcasted_iota(jnp.int32, (rows, group_tok), 1).astype(jnp.float32)
        take[e] = (at == token).astype(jnp.float32).astype(jnp.bfloat16)

    def select(e, q):
        return jnp.dot(take[e], group[q], preferred_element_type=jnp.float32).astype(jnp.bfloat16)

    sends, sends_s, moved_s = {}, {}, {}
    crossed, moved, turned, pairs, middle, last, ends = {}, {}, {}, {}, {}, {}, []
    seen = set()
    score_acc[...] = jnp.zeros_like(score_acc)

    def once(*key):
        new = key not in seen
        seen.add(key)
        return new

    def csend(k, h):
        if once("own"):
            own_copies[1].wait()
        if once("first", h):
            for j in (2, 3, 1):
                first[j, h].wait_recv()
        e = expert_at[k]
        out_x[k - half, :, halves[h]] = jnp.dot(
            take[e], group[y, :, halves[h]], preferred_element_type=jnp.float32
        ).astype(jnp.bfloat16)
        sends[k, h] = remote_to(
            out_x.at[k - half, :, halves[h]], fetched.at[g, :, cols(s, h)], (e, s)
        )
        sends[k, h].start()

    def ssend(k, i):
        if once("own"):
            own_copies[1].wait()
        if i == 0:
            for h in range(PIECES):
                if once("first", h):
                    for j in (2, 3, 1):
                        first[j, h].wait_recv()
        elif once("second"):
            for d in second:
                d.wait_recv()
            own_copies[2].wait()
        e = expert_at[k]
        if k:
            here = pl.ds(i * width, width)
            out_s[k, :, here] = select(e, side[i])
            sends_s[k, i] = remote_to(
                out_s.at[k, :, here], fetched.at[g, :, columns(flip(s, 2 * i), width)], (e, s)
            )
            sends_s[k, i].start()
        else:
            fetched[g, :, columns(flip(s, 2 * i), width)] = select(e, side[i])

    def mix(n):
        if n + 1 < len(raw_copies):
            raw_copies[n + 1].start()
        raw_copies[n].wait()
        _, dst, i = raw_parts[n]
        dst[i * step_rows : (i + 1) * step_rows, :] = raw[n % 2].reshape(
            step_rows, 2 * hidden_part
        )

    def place():
        ids_here = chosen[...]
        low = row * group_tok
        hits = (ids_here >= low) & (ids_here < low + group_tok)
        rank[2] = jnp.where(hits, running_count(hits) - 1.0, -1.0)

        @pl.loop(0, n_exp)
        def _(e):
            picked = rank[2, pl.ds(e, 1), :] == slot
            place1[e] = picked.astype(jnp.float32).astype(jnp.bfloat16)
            weight[e] = jnp.sum(jnp.where(picked, scores[...], 0.0), axis=1, keepdims=True)
            pre_pad[e] = jnp.dot(
                place1[e], pre[...], preferred_element_type=jnp.float32
            ).astype(jnp.bfloat16)

    def taket():
        @pl.loop(0, 2)
        def _(h):
            at = spot[pl.ds(h * half, half)].reshape(half * rows, 1)
            a = lax.broadcasted_iota(jnp.int32, (half * rows, half * rows), 0)
            b = lax.broadcasted_iota(jnp.int32, (half * rows, half * rows), 1)
            flat = jnp.sum(jnp.where(a == b, at, 0.0), axis=0, keepdims=True)
            token = lax.broadcasted_iota(jnp.int32, (group_tok, half * rows), 0)
            token = token.astype(jnp.float32)
            take_t[h] = (token == flat).astype(jnp.float32).astype(jnp.bfloat16)

    def ready():
        get_down.wait()

    def fwd(k, i):
        if k:
            sends_s[k, i].wait_recv()
        block = fetched.at[expert_at[k], :, columns(flip(s, 2 * i), width)]
        moved_s[k, i] = remote_to(block, block, beside)
        moved_s[k, i].start()

    def spread(k, h):
        block = fetched.at[expert_at[k], :, cols(s, h)]
        sends[k, h].wait_recv()
        crossed[k, h] = remote_to(block, block, across)
        crossed[k, h].start()
        moved[k, h] = remote_to(block, block, beside)
        moved[k, h].start()

    def turn(k, h):
        block = fetched.at[expert_at[k], :, cols(flip(s, 2), h)]
        crossed[k, h].wait_recv()
        turned[k, h] = remote_to(block, block, beside)
        turned[k, h].start()

    def compute(k):
        e = expert_at[k]
        if k < half:
            for i in range(2):
                moved_s[k, i].wait_recv()
        else:
            for h in range(PIECES):
                moved[k, h].wait_recv()
                turned[k, h].wait_recv()
        back = lax.dot_general(
            fetched[e], down[...], (((1,), (1,)), ((), ())), preferred_element_type=jnp.float32
        )
        gate_pre = pre_pad[e, :, :hidden_part].astype(jnp.float32)
        up_pre = pre_pad[e, :, hidden_part:].astype(jnp.float32)
        sigmoid_gate = jax.nn.sigmoid(gate_pre)
        activated = gate_pre * sigmoid_gate
        hidden = (activated * up_pre).astype(jnp.bfloat16)
        value = jnp.sum(hidden.astype(jnp.float32) * back, axis=1, keepdims=True)
        here = place1[e].astype(jnp.float32) > 0.5
        score_acc[...] += jnp.sum(jnp.where(here, value, 0.0), axis=0, keepdims=True)
        scaled = weight[e] * back
        d_gate = scaled * up_pre * sigmoid_gate * (1.0 + gate_pre * (1.0 - sigmoid_gate))
        both[:, :hidden_part] = d_gate.astype(jnp.bfloat16)
        both[:, hidden_part:] = (scaled * activated).astype(jnp.bfloat16)

        p = e % half
        copies = {}
        for bits in (3, 1, 2, 0):
            quarter = flip(s, bits)

            @pl.loop(0, width // 512)
            def _(i):
                tile = pl.ds(pl.multiple_of(quarter * width + i * 512, 512), 512)
                part[e, :, tile] = lax.dot_general(
                    both[...],
                    mixing[tile, :],
                    (((1,), (1,)), ((), ())),
                    preferred_element_type=jnp.float32,
                ).astype(jnp.bfloat16)

            if bits % 2:
                if k < half:
                    here = near_s.at[p, :, pl.ds(bits // 2 * width, width)]
                else:
                    here = near.at[p, 1 - bits // 2]
                copies[bits] = remote_to(part.at[e, :, columns(quarter, width)], here, beside)
                copies[bits].start()
        pairs[k] = [copies[1], copies[3]] if k < half else [copies[3], copies[1]]

    def gives(k, i):
        e = expert_at[k]
        p = e % half
        here = pl.ds(i * width, width)
        pairs[k][i].wait_recv()
        value = part[e, :, columns(flip(s, 2 * i), width)].astype(jnp.float32)
        value = (value + near_s[p, :, here].astype(jnp.float32)).astype(jnp.bfloat16)
        if k:
            sends_s[k, i].wait_send()
            out_s[k, :, here] = value
            last[k, i] = remote_to(out_s.at[k, :, here], arrived_s.at[pg, :, here], (e, s))
            last[k, i].start()
        else:
            arrived_s[pg, :, here] = value

    def hand(k, h):
        e = expert_at[k]
        p = e % half
        if once("pair", k, 0):
            pairs[k][0].wait_recv()
        sends[k, h].wait_send()
        value = part[e, :, cols(flip(s, 2), h)].astype(jnp.float32)
        value = value + near[p, 0, :, halves[h]].astype(jnp.float32)
        out_x[k - half, :, halves[h]] = value.astype(jnp.bfloat16)
        middle[k, h] = remote_to(
            out_x.at[k - half, :, halves[h]], far.at[p, :, halves[h]], across
        )
        middle[k, h].start()

    def give(k, h):
        e = expert_at[k]
        p = e % half
        if once("pair", k, 1):
            pairs[k][1].wait_recv()
        middle[k, h].wait_recv()
        value = part[e, :, cols(s, h)].astype(jnp.float32)
        value = value + near[p, 1, :, halves[h]].astype(jnp.float32)
        value = value + far[p, :, halves[h]].astype(jnp.float32)
        sum2[p, :, halves[h]] = value.astype(jnp.bfloat16)
        last[k, h] = remote_to(
            sum2.at[p, :, halves[h]], arrived_x.at[pg, :, halves[h]], (e, s)
        )
        last[k, h].start()

    def score():
        for j in range(1, 4):
            ends.append(remote_to(score_acc, score_out.at[s], (g, seq_at[j])))
            ends[-1].start()
        ends.append(local_copy(score_acc, score_out.at[s]))
        ends[-1].start()

    def token_block(j):
        return pl.ds(pl.multiple_of(seq_at[j] * own_tok, own_tok), own_tok)

    def finish_s():
        for j in range(1, half):
            last[j, 1].wait_recv()
        terms = arrived_s[:, :, width:].reshape(half * rows, width)
        group[0] = jnp.dot(
            take_t[hg], terms, preferred_element_type=jnp.float32
        ).astype(jnp.bfloat16)
        for j in (2, 3, 1, 0):
            src = group.at[0, token_block(j)]
            dst = same_out.at[:, theirs]
            ends.append(remote_to(src, dst, (g, seq_at[j])) if j else local_copy(src, dst))
            ends[-1].start()

    def finish_x(h):
        if once("near"):
            for j in range(1, half):
                last[j, 0].wait_recv()
        for j in range(half, n_exp):
            last[j, h].wait_recv()
        terms = arrived_x[:, :, halves[h]].reshape(half * rows, hw)
        value = jnp.dot(take_t[1 - hg], terms, preferred_element_type=jnp.float32)
        terms = arrived_s[:, :, halves[h]].reshape(half * rows, hw)
        value = value + jnp.dot(take_t[hg], terms, preferred_element_type=jnp.float32)
        acc_x[:, halves[h]] = value.astype(jnp.bfloat16)
        for j in (2, 3, 1, 0):
            src = acc_x.at[token_block(j), halves[h]]
            dst = cross_out.at[:, cols(s, h)]
            ends.append(remote_to(src, dst, (g, seq_at[j])) if j else local_copy(src, dst))
            ends[-1].start()

    steps = {
        "csend": csend, "ssend": ssend, "mix": mix, "place": place, "taket": taket, "ready": ready,
        "fwd": fwd, "spread": spread, "turn": turn, "compute": compute, "gives": gives,
        "hand": hand, "give": give, "score": score, "finish_s": finish_s, "finish_x": finish_x,
    }
    for step, numbers in plan():
        steps[step](*numbers)
    for d in id_sends + second:
        d.wait_send()
    for group_of in (first, crossed, moved, turned, moved_s, middle, last):
        for d in group_of.values():
            d.wait_send()
    for k in range(n_exp):
        for d in pairs[k]:
            d.wait_send()
    for d in ends:
        d.wait()


def layer(n_exp, out_grad, chosen, scores, pre, mixing, down):
    own_tok, model_width = out_grad.shape
    capacity = chosen.shape[1]
    width = model_width // 4
    group_tok = own_tok * 4
    rows = 9 * capacity // (8 * n_exp)
    half = n_exp // 2
    hidden2 = 2 * mixing.shape[2]
    step_rows = 512
    kind = out_grad.dtype
    dma = pltpu.SemaphoreType.DMA
    f32 = jnp.float32

    def v(*shape, dtype=kind):
        return pltpu.VMEM(shape, dtype)

    total = 30 * PIECES + 60
    return pl.pallas_call(
        functools.partial(layer_kernel, n_exp, group_tok),
        out_shape=(
            jax.ShapeDtypeStruct((own_tok, model_width), kind),
            jax.ShapeDtypeStruct((own_tok, model_width), kind),
            jax.ShapeDtypeStruct((4, 1, capacity), f32),
        ),
        in_specs=[ANY, VMEM, VMEM, ANY, ANY, ANY],
        out_specs=(ANY, ANY, VMEM),
        scratch_shapes=[
            v(n_exp, 1, capacity, dtype=jnp.int32),
            v(2, group_tok, width),
            v(3, n_exp, capacity, dtype=f32),
            v(n_exp, rows, capacity),
            v(n_exp, rows, 1, dtype=f32),
            v(n_exp, rows, group_tok),
            v(2, group_tok, half * rows),
            v(n_exp, rows, 1, dtype=f32),
            v(capacity, hidden2),
            v(n_exp, rows, hidden2),
            v(model_width, hidden2),
            v(hidden2 // 2, model_width),
            v(2, step_rows, 2, hidden2 // 2),
            v(n_exp, rows, model_width),
            v(rows, hidden2),
            v(n_exp, rows, model_width),
            v(half, rows, 2 * width),
            v(half, rows, width),
            v(half, rows, 2 * width),
            v(half, 2, rows, width),
            v(half, rows, width),
            v(half, rows, width),
            v(half, rows, 2 * width),
            v(half, rows, width),
            v(group_tok, width),
            v(1, capacity, dtype=f32),
            dma((24,)),
            dma((total,)),
            dma((total,)),
        ],
        compiler_params=pltpu.CompilerParams(
            collective_id=4, has_side_effects=True, vmem_limit_bytes=60 * 2**20
        ),
    )(out_grad, chosen, scores, pre, mixing, down)


def regroup_kernel(
    n_seq, totals, score, out, score_sum, scores, send, recv, send_s, recv_s, local
):
    g, s = lax.axis_index("exp"), lax.axis_index("seq")
    width = totals.shape[2]
    own = columns(s, width)
    greet([(g, flip(s, k)) for k in range(1, n_seq)])
    copies = []
    for k in range(n_seq - 1, 0, -1):
        t = flip(s, k)
        copies.append(remote(totals.at[t], out.at[:, own], send.at[k], recv.at[k], (g, t)))
        copies[-1].start()
        copies.append(remote(score, scores.at[s], send_s.at[k], recv_s.at[k], (g, t)))
        copies[-1].start()
    mine = pltpu.make_async_copy(totals.at[s], out.at[:, own], local)
    mine.start()
    scores[s] = score[...]
    for c in copies:
        c.wait()
    value = scores[0]
    for k in range(1, n_seq):
        value = value + scores[k]
    score_sum[...] = value
    mine.wait()


def regroup(n_seq, totals, score):
    rows, width = totals.shape[1:]
    dma = pltpu.SemaphoreType.DMA
    return pl.pallas_call(
        functools.partial(regroup_kernel, n_seq),
        out_shape=(
            jax.ShapeDtypeStruct((rows, n_seq * width), totals.dtype),
            jax.ShapeDtypeStruct(score.shape, score.dtype),
        ),
        in_specs=[VMEM, VMEM],
        out_specs=(VMEM, VMEM),
        scratch_shapes=[pltpu.VMEM((n_seq,) + score.shape, score.dtype)]
        + [dma((n_seq,))] * 4
        + [dma],
        compiler_params=pltpu.CompilerParams(collective_id=3, has_side_effects=True),
    )(totals, score)


def counts(hits):
    length = hits.shape[1]
    at = jnp.arange(length, dtype=jnp.int32)
    upper = (at[:, None] <= at[None, :]).astype(jnp.bfloat16)
    total = jnp.dot(hits.astype(jnp.bfloat16), upper, preferred_element_type=jnp.float32)
    return total.astype(jnp.int32)


def local(out_grad, chosen, scores, saved_pre, gate_up, down):
    n_exp = lax.axis_size("exp")
    n_seq = lax.axis_size("seq")
    capacity = chosen.shape[1]
    slot_most = 9 * capacity // (8 * n_exp)
    tok_count, model_width = out_grad.shape
    width = model_width // n_seq
    group_tok = tok_count * n_seq
    pad_rows = n_exp * slot_most
    hidden_part = gate_up.shape[3]
    group_index = lax.axis_index("exp")

    if slot_most % 16 == 0 and n_exp == 8 and n_seq == 4:
        same, cross, score_parts = layer(
            n_exp,
            out_grad,
            chosen,
            scores,
            saved_pre[0],
            gate_up[0],
            down[0],
        )
        value = same.astype(jnp.float32) + cross.astype(jnp.float32)
        return value.astype(jnp.bfloat16), jnp.sum(score_parts, axis=0)

    own_ids = chosen[0]
    owner_group = own_ids // group_tok
    owner_hits = (owner_group[None, :] == jnp.arange(n_exp, dtype=jnp.int32)[:, None]).astype(
        jnp.int32
    )
    slot_order = jnp.sum(counts(owner_hits) * owner_hits, axis=0) - 1
    position = owner_group * slot_most + slot_order
    place = position[None, :] == jnp.arange(pad_rows, dtype=jnp.int32)[:, None]
    weight_padded = jnp.sum(jnp.where(place, scores[0][None, :], 0.0), axis=1)
    place_one = place.astype(jnp.bfloat16)

    def padded(x):
        return jnp.dot(place_one, x, preferred_element_type=jnp.float32)

    gate_pre = padded(saved_pre[0, :, 0])
    up_pre = padded(saved_pre[0, :, 1])
    mixing = gate_up[0].reshape(model_width, 2 * hidden_part)

    ids, group = exchange(n_exp, n_seq, chosen.reshape(capacity // 128, 128), out_grad)
    local_ids = ids.reshape(n_exp, capacity) - group_index * group_tok
    inside = (local_ids >= 0) & (local_ids < group_tok)
    slot_rank = counts(inside) - 1
    slot_ids = jnp.arange(slot_most, dtype=jnp.int32)
    picked = inside[:, None, :] & (slot_rank[:, None, :] == slot_ids[None, :, None])
    source = jnp.sum(jnp.where(picked, local_ids[:, None, :] + 1, 0), axis=2).reshape(pad_rows) - 1
    tokens = jnp.arange(group_tok, dtype=jnp.int32)
    take = (source[:, None] == tokens[None, :]).astype(jnp.bfloat16)
    outgoing = jnp.dot(
        take, group.reshape(group_tok, width), preferred_element_type=jnp.float32
    ).astype(jnp.bfloat16)
    outgoing = outgoing.reshape(n_exp, slot_most, width)
    fetched = dispatch(n_exp, n_seq, outgoing)
    fetched = fetched.reshape(pad_rows, model_width)

    back_grad = lax.dot_general(
        fetched, down[0], (((1,), (1,)), ((), ())), preferred_element_type=jnp.float32
    )
    sigmoid_gate = jax.nn.sigmoid(gate_pre)
    activated = gate_pre * sigmoid_gate
    hidden = (activated * up_pre).astype(jnp.bfloat16)
    hidden = lax.optimization_barrier(hidden)
    score_part = jnp.sum(hidden.astype(jnp.float32) * back_grad, axis=1)
    scaled = weight_padded[:, None] * back_grad
    d_gate = scaled * up_pre * sigmoid_gate * (1.0 + gate_pre * (1.0 - sigmoid_gate))
    d_up = scaled * activated
    d_both = jnp.concatenate([d_gate, d_up], axis=1).astype(jnp.bfloat16)
    partial_value = lax.dot_general(
        d_both, mixing, (((1,), (1,)), ((), ())), preferred_element_type=jnp.float32
    ).astype(jnp.bfloat16)
    arrived = combine(n_exp, n_seq, partial_value.reshape(n_exp, slot_most, model_width))
    score_slots = jnp.sum(jnp.where(place, score_part[:, None], 0.0), axis=0)
    totals = lax.dot_general(
        take,
        arrived.reshape(pad_rows, width),
        (((0,), (0,)), ((), ())),
        preferred_element_type=jnp.float32,
    ).astype(jnp.bfloat16)
    summed, score_grad = regroup(
        n_seq,
        totals.reshape(n_seq, tok_count, width),
        score_slots.reshape(capacity // 128, 128),
    )
    return (summed, score_grad.reshape(1, capacity))


def solution(mesh):
    return jax.shard_map(
        local,
        mesh=mesh,
        in_specs=(
            P(("exp", "seq"), None),
            P("exp", None),
            P("exp", None),
            P("exp", None, None, "seq"),
            P("exp", None, None, "seq"),
            P("exp", "seq", None),
        ),
        out_specs=(P(("exp", "seq"), None), P("exp", None)),
        check_vma=False,
    )
```
